256 devices in a mesh: member: 8 (over x, z_hi), rows: 32 (over y, z_lo, core).
Axes of the slice: x: 4, y: 4, z: 8 (z_hi: 2, z_lo: 4; z = z_hi * 4 + z_lo), core: 2. Of those that a mesh axis runs over, the one named last changes fastest.
Arguments:
- member_latent_state: bfloat16 [16, 128, 64, 512], P('member', 'rows'), as said below
- analysis_target_field: bfloat16 [128, 64, 512], P('rows'), may hold values from -8 to 8
- conv_first: bfloat16 [512, 9, 512], replicated, may hold values from -0.09375 to 0.09375
- second_kernel_weight: bfloat16 [512, 9, 512], replicated, may hold values from -0.09375 to 0.09375
Outputs:
- ensemble_prognosis_field: bfloat16 [16, 128, 64, 512], P('member', 'rows')
- initial_conv_derivative: float32 [512, 9, 512], P('rows')
- final_filter_slope: float32 [512, 9, 512], P('rows')
The draws below stay inside these ranges and needn't reach their ends.
Inputs may be any that keep to these rules, and one draw needn't show every extreme that they name: `member_latent_state`: each member's field is drawn independently.
All inputs are finite; a program needn't handle non-finite values.
Results may differ from the reference program's by a relative error of at most 0.0058.
Values may be sent and summed in bfloat16 or wider, within the bound.
A program may use at most 192 MiB of HBM per device.

```python
import jax
import jax.numpy as jnp
from jax import lax

C = 512
COLS = 64
MEMBERS = 16
NROWS = 128


def draw_member_latent_state(key, part):
    dims_full = (MEMBERS, NROWS, COLS, C)
    position = jnp.arange(NROWS, dtype=jnp.float32) / float(max(NROWS - 1, 1))
    values_raw = jax.random.normal(key, dims_full, jnp.float32)
    amplitude = jnp.power(3.0, position)
    return (values_raw * amplitude[None, :, None, None]).astype(jnp.bfloat16)


def steps_of(key, dims, shards, least, top_value):
    gain = 1.0
    for dim, shards_of in shards:
        steps = jax.random.uniform(jax.random.fold_in(jax.random.fold_in(key, 6), dim), (shards_of,), jnp.float32, least / len(shards), top_value / len(shards))
        gain = gain * jnp.repeat(jnp.exp(steps), dims[dim] // shards_of).reshape((-1,) + (1,) * (len(dims) - 1 - dim))
    return gain


def bell_draw(rng, dims, width, bound, split=(), kind=jnp.bfloat16):
    gain = steps_of(rng, dims, split, -0.22, 0.18) if split else 1.0
    values = jax.random.normal(rng, dims, jnp.float32) * width * gain
    return jnp.minimum(jnp.maximum(values, -bound), bound).astype(kind)


def setup_inputs(seed: int = 0) -> dict:
    arg_keys = jax.random.split(jax.random.key(seed), 5)
    return {
        "member_latent_state": draw_member_latent_state(jax.random.fold_in(arg_keys[4], 71), 0),
        "analysis_target_field": bell_draw(arg_keys[1], (NROWS, COLS, C), 1.5, 8.0, ((0, 32),)),
        "conv_first": bell_draw(arg_keys[2], (C, 9, C), (9 * C) ** -0.5, 0.09375),
        "second_kernel_weight": bell_draw(arg_keys[3], (C, 9, C), (9 * C) ** -0.5, 0.09375),
    }


SOFTENING_EPS = 0.1
INV_ROOT_TWO = 0.7071067811865476
INV_ROOT_TWOPI = 0.3989422804014327

def gelu_value(pre):
    return 0.5 * pre * (1.0 + lax.erf(pre * INV_ROOT_TWO))

def gelu_slope(pre):
    return 0.5 * (1.0 + lax.erf(pre * INV_ROOT_TWO)) + pre * jnp.exp(-0.5 * pre * pre) * INV_ROOT_TWOPI

def zero_extend_field(field):
    return jnp.pad(field, ((0, 0), (1, 1), (1, 1), (0, 0)))

def tap_view(padded, tap_index, meridian_extent, longitude_length):
    down = tap_index // 3
    across = tap_index % 3
    return padded[:, down:down + meridian_extent, across:across + longitude_length, :]

def apply_kernel_stencil(padded, kernel, meridian_extent, longitude_length):
    channels = padded.shape[3]
    summed = jnp.zeros((padded.shape[0] * meridian_extent * longitude_length, kernel.shape[2]), jnp.float32)
    for tap_index in range(9):
        view = tap_view(padded, tap_index, meridian_extent, longitude_length).reshape(-1, channels)
        summed = summed + jnp.dot(view, kernel[:, tap_index, :], preferred_element_type=jnp.float32)
    return summed.reshape(padded.shape[0], meridian_extent, longitude_length, kernel.shape[2])

def reversed_stencil(padded, kernel, meridian_extent, longitude_length):
    channels = padded.shape[3]
    summed = jnp.zeros((padded.shape[0] * meridian_extent * longitude_length, kernel.shape[0]), jnp.float32)
    for tap_index in range(9):
        view = tap_view(padded, 8 - tap_index, meridian_extent, longitude_length).reshape(-1, channels)
        summed = summed + jnp.dot(view, kernel[:, tap_index, :].T, preferred_element_type=jnp.float32)
    return summed.reshape(padded.shape[0], meridian_extent, longitude_length, kernel.shape[0])

def stencil_derivative(padded, cotangent, meridian_extent, longitude_length):
    channels = padded.shape[3]
    flat_cot = cotangent.reshape(-1, cotangent.shape[3])
    taps_list = []
    for tap_index in range(9):
        view = tap_view(padded, tap_index, meridian_extent, longitude_length).reshape(-1, channels)
        taps_list.append(jnp.dot(view.T, flat_cot, preferred_element_type=jnp.float32))
    return jnp.stack(taps_list, axis=1)

def attraction_sum(local, everyone):

    def step(running, other):
        spread = local - other[None]
        smooth_abs = jnp.sqrt(spread * spread + SOFTENING_EPS * SOFTENING_EPS)
        return (running + spread / smooth_abs, None)
    result, unused = lax.scan(step, jnp.zeros(local.shape, jnp.float32), everyone)
    return result

def reference(member_latent_state, analysis_target_field, conv_first, second_kernel_weight):
    meridian_extent = member_latent_state.shape[1]
    longitude_length = member_latent_state.shape[2]
    count_members = member_latent_state.shape[0]
    padded_state = zero_extend_field(member_latent_state)
    pre_first = apply_kernel_stencil(padded_state, conv_first, meridian_extent, longitude_length)
    hidden = gelu_value(pre_first).astype(jnp.bfloat16)
    hidden_state_bordered = zero_extend_field(hidden)
    model_output_field = member_latent_state.astype(jnp.float32) + apply_kernel_stencil(hidden_state_bordered, second_kernel_weight, meridian_extent, longitude_length)
    ensemble_prognosis_field = model_output_field.astype(jnp.bfloat16)
    prognosis_misfit = model_output_field - analysis_target_field.astype(jnp.float32)[None]
    distance_to_analysis = jnp.sqrt(prognosis_misfit * prognosis_misfit + SOFTENING_EPS * SOFTENING_EPS)
    pairwise_spread_part = attraction_sum(model_output_field, model_output_field)
    ensemble_draw_count = float(count_members)
    output_cotangent_field = ((prognosis_misfit / distance_to_analysis / ensemble_draw_count - pairwise_spread_part / (ensemble_draw_count * (ensemble_draw_count - 1.0))) / float(meridian_extent)).astype(jnp.bfloat16)
    final_filter_slope = stencil_derivative(hidden_state_bordered, output_cotangent_field, meridian_extent, longitude_length)
    intermediate_adjoint = reversed_stencil(zero_extend_field(output_cotangent_field), second_kernel_weight, meridian_extent, longitude_length)
    cot_pre = (intermediate_adjoint * gelu_slope(pre_first)).astype(jnp.bfloat16)
    initial_conv_derivative = stencil_derivative(padded_state, cot_pre, meridian_extent, longitude_length)
    return (ensemble_prognosis_field, initial_conv_derivative, final_filter_slope)
```

```python
import functools

import jax
import jax.numpy as jnp
from jax import lax
from jax.experimental import pallas as pl
from jax.experimental.pallas import tpu as pltpu
from jax.sharding import PartitionSpec as P

MESH = pl.DeviceIdType.MESH
EPS2 = 0.1 * 0.1
INV_ROOT_TWO = 0.7071067811865476
INV_ROOT_TWOPI = 0.3989422804014327


def gelu_value(pre):
    return 0.5 * pre * (1.0 + lax.erf(pre * INV_ROOT_TWO))


def gelu_slope(pre):
    return 0.5 * (1.0 + lax.erf(pre * INV_ROOT_TWO)) + pre * jnp.exp(-0.5 * pre * pre) * INV_ROOT_TWOPI


def padded(field):
    count = lax.axis_size("rows")
    forward = [(i, i + 1) for i in range(count - 1)]
    backward = [(b, a) for a, b in forward]
    low = lax.ppermute(field[:, -1:], "rows", forward)
    high = lax.ppermute(field[:, :1], "rows", backward)
    field = jnp.concatenate([low, field, high], axis=1)
    return jnp.pad(field, ((0, 0), (0, 0), (1, 1), (0, 0)))


def tap_view(pad, tap, rows, cols):
    return pad[:, tap // 3 : tap // 3 + rows, tap % 3 : tap % 3 + cols, :].reshape(-1, pad.shape[3])


def conv(pad, kernel, rows, cols):
    total = 0.0
    for tap in range(9):
        total = total + jnp.dot(tap_view(pad, tap, rows, cols), kernel[:, tap, :], preferred_element_type=jnp.float32)
    return total.reshape(pad.shape[0], rows, cols, kernel.shape[2])


def adjoint(pad, kernel, rows, cols):
    total = 0.0
    for tap in range(9):
        total = total + lax.dot_general(
            tap_view(pad, 8 - tap, rows, cols),
            kernel[:, tap, :],
            (((1,), (1,)), ((), ())),
            preferred_element_type=jnp.float32,
        )
    return total.reshape(pad.shape[0], rows, cols, kernel.shape[0])


def tap_terms(pad, cot, rows, cols):
    flat = cot.reshape(-1, cot.shape[3])
    terms = []
    for tap in range(9):
        terms.append(
            lax.dot_general(
                tap_view(pad, tap, rows, cols), flat, (((0,), (0,)), ((), ())), preferred_element_type=jnp.float32
            ).astype(jnp.bfloat16)
        )
    return jnp.stack(terms, axis=0)


SUB = 2


def score_kernel(f_ref, t_ref, out_ref, everyone, cots, s1, r1, s2, r2):
    member, rows = lax.axis_index("member"), lax.axis_index("rows")
    cells = everyone.shape[1]
    width = cells // SUB

    def peer(k):
        return {"member": lax.rem(member + k, 8), "rows": rows}

    barrier = pltpu.get_barrier_semaphore()
    for k in range(1, 8):
        pl.semaphore_signal(barrier, inc=1, device_id=peer(k), device_id_type=MESH)
    pl.semaphore_wait(barrier, 7)

    def out_copy(s, k):
        to = lax.rem(member + k, 8)
        start = pl.multiple_of(to * cells + s * width, 8)
        return pltpu.make_async_remote_copy(
            src_ref=f_ref.at[:, pl.ds(start, width)],
            dst_ref=everyone.at[pl.ds(member * 2, 2), pl.ds(s * width, width)],
            send_sem=s1.at[s, k],
            recv_sem=r1.at[s, k],
            device_id=peer(k),
            device_id_type=MESH,
        )

    def back_copy(s, k):
        to = lax.rem(member + k, 8)
        start = pl.multiple_of(member * cells + s * width, 8)
        return pltpu.make_async_remote_copy(
            src_ref=cots.at[pl.ds(to * 2, 2), pl.ds(s * width, width)],
            dst_ref=out_ref.at[:, pl.ds(start, width)],
            send_sem=s2.at[s, k],
            recv_sem=r2.at[s, k],
            device_id=peer(k),
            device_id_type=MESH,
        )

    for s in range(SUB):
        for k in (4, 3, 5, 1, 7, 2, 6):
            out_copy(s, k).start()
    mine = pl.multiple_of(member * cells, 8)
    everyone[pl.ds(member * 2, 2)] = f_ref[:, pl.ds(mine, cells)]
    for s in range(SUB):
        for k in range(1, 8):
            out_copy(s, k).wait_recv()

        @pl.loop(0, width // 16)
        def _(c):
            start = pl.multiple_of(s * width + c * 16, 16)
            tstart = pl.multiple_of(mine + s * width + c * 16, 16)
            for lane in range(0, 512, 128):
                spot = (pl.ds(start, 16), pl.ds(lane, 128))
                truth = t_ref[pl.ds(tstart, 16), pl.ds(lane, 128)].astype(jnp.float32)
                xs = [everyone[(k,) + spot] for k in range(16)]
                pulls = [None] * 16

                def plus(i, v):
                    pulls[i] = v if pulls[i] is None else pulls[i] + v

                for a in range(16):
                    for b in range(a + 1, 16):
                        d = xs[a] - xs[b]
                        u = d * lax.rsqrt(d * d + EPS2)
                        plus(a, u)
                        plus(b, -u)
                for k in range(16):
                    d = xs[k] - truth
                    slope = d * lax.rsqrt(d * d + EPS2)
                    cots[(k,) + spot] = (slope * (1.0 / 2048.0) - pulls[k] * (1.0 / 30720.0)).astype(jnp.bfloat16)

        for k in (4, 3, 5, 1, 7, 2, 6):
            back_copy(s, k).start()
    out_ref[:, pl.ds(mine, cells)] = cots[pl.ds(member * 2, 2)]
    for s in range(SUB):
        for k in range(1, 8):
            out_copy(s, k).wait_send()
            back_copy(s, k).wait()


def score(forecast, truth):
    members, cells, channels = forecast.shape
    part = cells // 8
    return pl.pallas_call(
        score_kernel,
        out_shape=jax.ShapeDtypeStruct(forecast.shape, jnp.bfloat16),
        in_specs=[pl.BlockSpec(memory_space=pltpu.VMEM)] * 2,
        out_specs=pl.BlockSpec(memory_space=pltpu.VMEM),
        scratch_shapes=[
            pltpu.VMEM((members * 8, part, channels), jnp.float32),
            pltpu.VMEM((members * 8, part, channels), jnp.bfloat16),
        ]
        + [pltpu.SemaphoreType.DMA((SUB, 8))] * 4,
        compiler_params=pltpu.CompilerParams(collective_id=0, has_side_effects=True, vmem_limit_bytes=32 << 20),
        name="score",
    )(forecast, truth)


def reduce_kernel(ga, gb, outa, outb, cr, sa, ra, sb, rb, ta, tra, tb, trb, u, ur, v, vr, fin, *sems):
    s0, r0, s1, r1, s2, r2, s3, r3, s4, r4, s5, r5 = sems
    member, rows = lax.axis_index("member"), lax.axis_index("rows")
    x, zh = member // 2, lax.rem(member, 2)
    y, z, c = rows // 8, lax.rem(rows // 2, 4), lax.rem(rows, 2)
    grads, outs = (ga, gb), (outa, outb)

    def at(px, pzh, py, pz, pc):
        return {"member": px * 2 + pzh, "rows": (py * 4 + pz) * 2 + pc}

    sibling = at(x, zh, y, z, 1 - c)
    far = at(x, 1 - zh, y, z, c)

    def along_y(k):
        return at(x, zh, lax.rem(y + k, 4), z, c)

    def along_x(k):
        return at(lax.rem(x + k, 4), zh, y, z, c)

    def along_z(k):
        return at(x, zh, y, lax.rem(z + k, 4), c)

    def send(src, dst, ssem, rsem, to):
        return pltpu.make_async_remote_copy(
            src_ref=src, dst_ref=dst, send_sem=ssem, recv_sem=rsem, device_id=to, device_id_type=MESH
        )

    barrier = pltpu.get_barrier_semaphore()
    peers = [sibling, far] + [a(k) for a in (along_y, along_x, along_z) for k in (1, 2, 3)]
    for p in peers:
        pl.semaphore_signal(barrier, inc=1, device_id=p, device_id_type=MESH)
    pl.semaphore_wait(barrier, len(peers))

    def step0(g):
        return send(grads[g].at[:, :, 1 - c], cr.at[g], s0.at[g], r0.at[g], sibling)

    def step1(g, h, k):
        s, r = (sa, ra) if h == 0 else (sb, rb)
        to = lax.rem((y if h == 0 else x) + k, 4)
        return send(
            s.at[g, to], r.at[g, k - 1], s1.at[g, h, k], r1.at[g, h, k], along_y(k) if h == 0 else along_x(k)
        )

    def step2(g, h, k):
        s, r = (ta, tra) if h == 0 else (tb, trb)
        to = lax.rem((x if h == 0 else y) + k, 4)
        return send(
            s.at[g, to], r.at[g, k - 1], s2.at[g, h, k], r2.at[g, h, k], along_x(k) if h == 0 else along_y(k)
        )

    def step3(g, k):
        to = lax.rem(z + k, 4)
        return send(u.at[g, to], ur.at[g, k - 1], s3.at[g, k], r3.at[g, k], along_z(k))

    def step4(g):
        return send(v.at[g], vr.at[g], s4.at[g], r4.at[g], far)

    def step5(g, k):
        return send(fin.at[g, x], fin.at[g, x], s5.at[g, k], r5.at[g, k], along_x(k))

    for g in range(2):
        step0(g).start()

    for g in range(2):
        step0(g).wait_recv()

        @pl.loop(0, 9)
        def _(tap):
            @pl.loop(0, 4)
            def _(yy):
                for zz in range(4):
                    block = grads[g][tap, yy * 4 + zz, c].astype(jnp.float32) + cr[g, tap, yy * 4 + zz].astype(
                        jnp.float32
                    )
                    block = block.astype(jnp.bfloat16)
                    for xx in range(4):
                        piece = block[:, xx * 128 : (xx + 1) * 128]
                        if zz < 2:
                            sa[g, yy, xx, tap, zz] = piece
                        else:
                            sb[g, xx, yy, tap, zz - 2] = piece

        for k in (2, 1, 3):
            step1(g, 0, k).start()
            step1(g, 1, k).start()

    def summed(own, got, where):
        total = own[where].astype(jnp.float32)
        for k in range(3):
            total = total + got[(k,) + where].astype(jnp.float32)
        return total

    for g in range(2):
        for h in range(2):
            for k in (1, 2, 3):
                step1(g, h, k).wait_recv()
            own, got, into = ((sa, ra, ta), (sb, rb, tb))[h]
            here = y if h == 0 else x

            @pl.loop(0, 4)
            def _(other):
                @pl.loop(0, 9)
                def _(tap):
                    into[g, other, tap] = summed(own.at[g, here], got.at[g], (other, tap)).astype(jnp.bfloat16)

            for k in (2, 1, 3):
                step2(g, h, k).start()

    for g in range(2):
        for h in range(2):
            for k in (1, 2, 3):
                step2(g, h, k).wait_recv()
            own, got = ((ta, tra), (tb, trb))[h]
            here = x if h == 0 else y

            @pl.loop(0, 9)
            def _(tap):
                both = summed(own.at[g, here], got.at[g], (tap,)).astype(jnp.bfloat16)
                for zz in range(2):
                    u[g, h * 2 + zz, tap] = both[zz]

        for k in (2, 1, 3):
            step3(g, k).start()

    for g in range(2):
        for k in (1, 2, 3):
            step3(g, k).wait_recv()

        @pl.loop(0, 9)
        def _(tap):
            v[g, tap] = summed(u.at[g, z], ur.at[g], (tap,))

        step4(g).start()

    for g in range(2):
        step4(g).wait_recv()

        @pl.loop(0, 9)
        def _(tap):
            fin[g, x, tap] = v[g, tap] + vr[g, tap]

        for k in (2, 1, 3):
            step5(g, k).start()

    for g in range(2):
        for k in (1, 2, 3):
            step5(g, k).wait_recv()

        @pl.loop(0, 9)
        def _(tap):
            for xx in range(4):
                outs[g][tap, :, xx * 128 : (xx + 1) * 128] = fin[g, xx, tap]

    for g in range(2):
        step0(g).wait_send()
        step4(g).wait_send()
        for k in (1, 2, 3):
            for h in range(2):
                step1(g, h, k).wait_send()
                step2(g, h, k).wait_send()
            step3(g, k).wait_send()
            step5(g, k).wait_send()


def reduce_gradients(first, second):
    bf, f32 = jnp.bfloat16, jnp.float32
    shape = (9, 16, 2, 16, 512)
    dma = pltpu.SemaphoreType.DMA
    pair = [pltpu.VMEM((2, 4, 4, 9, 2, 16, 128), bf), pltpu.VMEM((2, 3, 4, 9, 2, 16, 128), bf)]
    quad = [pltpu.VMEM((2, 4, 9, 2, 16, 128), bf), pltpu.VMEM((2, 3, 9, 2, 16, 128), bf)]
    sems = []
    for dims in ((2,), (2, 2, 4), (2, 2, 4), (2, 4), (2,), (2, 4)):
        sems += [dma(dims), dma(dims)]
    outs = pl.pallas_call(
        reduce_kernel,
        out_shape=[jax.ShapeDtypeStruct((9, 16, 512), f32)] * 2,
        in_specs=[pl.BlockSpec(memory_space=pltpu.VMEM)] * 2,
        out_specs=[pl.BlockSpec(memory_space=pltpu.VMEM)] * 2,
        scratch_shapes=[pltpu.VMEM((2, 9, 16, 16, 512), bf)]
        + pair
        + pair
        + quad
        + quad
        + [
            pltpu.VMEM((2, 4, 9, 16, 128), bf),
            pltpu.VMEM((2, 3, 9, 16, 128), bf),
            pltpu.VMEM((2, 9, 16, 128), f32),
            pltpu.VMEM((2, 9, 16, 128), f32),
            pltpu.VMEM((2, 4, 9, 16, 128), f32),
        ]
        + sems,
        compiler_params=pltpu.CompilerParams(collective_id=1, has_side_effects=True, vmem_limit_bytes=56 << 20),
        name="reduce_gradients",
    )(first.reshape(shape), second.reshape(shape))
    return [jnp.transpose(o, (1, 0, 2)) for o in outs]


def body(state, truth, conv_first, conv_second):
    members, rows, cols, channels = state.shape
    state_pad = padded(state)
    pre = conv(state_pad, conv_first, rows, cols)
    hidden = gelu_value(pre).astype(jnp.bfloat16)
    hidden_pad = padded(hidden)
    forecast = state.astype(jnp.float32) + conv(hidden_pad, conv_second, rows, cols)
    prognosis = forecast.astype(jnp.bfloat16)
    cells = rows * cols
    cot = score(forecast.reshape(members, cells, channels), truth.reshape(cells, channels))
    cot = cot.reshape(members, rows, cols, channels)
    second_terms = tap_terms(hidden_pad, cot, rows, cols)
    back = adjoint(padded(cot), conv_second, rows, cols)
    cot_pre = (back * gelu_slope(pre)).astype(jnp.bfloat16)
    first_terms = tap_terms(state_pad, cot_pre, rows, cols)
    first_slope, second_slope = reduce_gradients(first_terms, second_terms)
    return prognosis, first_slope, second_slope


def solution(mesh):
    in_specs = (P("member", "rows", None, None), P("rows", None, None), P(), P())
    out_specs = (P("member", "rows", None, None), P("rows", None, None), P("rows", None, None))
    return jax.shard_map(body, mesh=mesh, in_specs=in_specs, out_specs=out_specs, check_vma=False)
```

```python
import functools

import jax
import jax.numpy as jnp
from jax import lax
from jax.experimental import pallas as pl
from jax.experimental.pallas import tpu as pltpu
from jax.sharding import PartitionSpec as P

MESH = pl.DeviceIdType.MESH
EPS2 = 0.1 * 0.1
INV_ROOT_TWO = 0.7071067811865476
INV_ROOT_TWOPI = 0.3989422804014327


def gelu_value(pre):
    return 0.5 * pre * (1.0 + lax.erf(pre * INV_ROOT_TWO))


def gelu_slope(pre):
    return 0.5 * (1.0 + lax.erf(pre * INV_ROOT_TWO)) + pre * jnp.exp(-0.5 * pre * pre) * INV_ROOT_TWOPI


def padded(field):
    count = lax.axis_size("rows")
    forward = [(i, i + 1) for i in range(count - 1)]
    backward = [(b, a) for a, b in forward]
    low = lax.ppermute(field[:, -1:], "rows", forward)
    high = lax.ppermute(field[:, :1], "rows", backward)
    field = jnp.concatenate([low, field, high], axis=1)
    return jnp.pad(field, ((0, 0), (0, 0), (1, 1), (0, 0)))


def tap_view(pad, tap, rows, cols):
    return pad[:, tap // 3 : tap // 3 + rows, tap % 3 : tap % 3 + cols, :].reshape(-1, pad.shape[3])


def conv(pad, kernel, rows, cols):
    total = 0.0
    for tap in range(9):
        total = total + jnp.dot(tap_view(pad, tap, rows, cols), kernel[:, tap, :], preferred_element_type=jnp.float32)
    return total.reshape(pad.shape[0], rows, cols, kernel.shape[2])


def column_shifts(pad, cols):
    ordered = jnp.transpose(pad, (1, 0, 2, 3))
    return jnp.stack([ordered[:, :, b : b + cols].reshape(-1, pad.shape[3]) for b in range(3)], axis=0)


SUB = 2


def score_kernel(f_ref, t_ref, out_ref, everyone, cots, s1, r1, s2, r2):
    member, rows = lax.axis_index("member"), lax.axis_index("rows")
    cells = everyone.shape[1]
    width = cells // SUB

    def peer(k):
        return {"member": lax.rem(member + k, 8), "rows": rows}

    barrier = pltpu.get_barrier_semaphore()
    for k in range(1, 8):
        pl.semaphore_signal(barrier, inc=1, device_id=peer(k), device_id_type=MESH)
    pl.semaphore_wait(barrier, 7)

    def out_copy(s, k):
        to = lax.rem(member + k, 8)
        start = pl.multiple_of(to * cells + s * width, 8)
        return pltpu.make_async_remote_copy(
            src_ref=f_ref.at[:, pl.ds(start, width)],
            dst_ref=everyone.at[pl.ds(member * 2, 2), pl.ds(s * width, width)],
            send_sem=s1.at[s, k],
            recv_sem=r1.at[s, k],
            device_id=peer(k),
            device_id_type=MESH,
        )

    def back_copy(s, k):
        to = lax.rem(member + k, 8)
        start = pl.multiple_of(member * cells + s * width, 8)
        return pltpu.make_async_remote_copy(
            src_ref=cots.at[pl.ds(to * 2, 2), pl.ds(s * width, width)],
            dst_ref=out_ref.at[:, pl.ds(start, width)],
            send_sem=s2.at[s, k],
            recv_sem=r2.at[s, k],
            device_id=peer(k),
            device_id_type=MESH,
        )

    for s in range(SUB):
        for k in (4, 3, 5, 1, 7, 2, 6):
            out_copy(s, k).start()
    mine = pl.multiple_of(member * cells, 8)
    everyone[pl.ds(member * 2, 2)] = f_ref[:, pl.ds(mine, cells)]
    for s in range(SUB):
        for k in range(1, 8):
            out_copy(s, k).wait_recv()

        @pl.loop(0, width // 16)
        def _(c):
            start = pl.multiple_of(s * width + c * 16, 16)
            tstart = pl.multiple_of(mine + s * width + c * 16, 16)
            for lane in range(0, 512, 128):
                spot = (pl.ds(start, 16), pl.ds(lane, 128))
                truth = t_ref[pl.ds(tstart, 16), pl.ds(lane, 128)].astype(jnp.float32)
                xs = [everyone[(k,) + spot] for k in range(16)]
                pulls = [None] * 16

                def plus(i, v):
                    pulls[i] = v if pulls[i] is None else pulls[i] + v

                for a in range(16):
                    for b in range(a + 1, 16):
                        d = xs[a] - xs[b]
                        u = d * lax.rsqrt(d * d + EPS2)
                        plus(a, u)
                        plus(b, -u)
                for k in range(16):
                    d = xs[k] - truth
                    slope = d * lax.rsqrt(d * d + EPS2)
                    cots[(k,) + spot] = (slope * (1.0 / 2048.0) - pulls[k] * (1.0 / 30720.0)).astype(jnp.bfloat16)

        for k in (4, 3, 5, 1, 7, 2, 6):
            back_copy(s, k).start()
    out_ref[:, pl.ds(mine, cells)] = cots[pl.ds(member * 2, 2)]
    for s in range(SUB):
        for k in range(1, 8):
            out_copy(s, k).wait_send()
            back_copy(s, k).wait()


def score(forecast, truth):
    members, cells, channels = forecast.shape
    part = cells // 8
    return pl.pallas_call(
        score_kernel,
        out_shape=jax.ShapeDtypeStruct(forecast.shape, jnp.bfloat16),
        in_specs=[pl.BlockSpec(memory_space=pltpu.VMEM)] * 2,
        out_specs=pl.BlockSpec(memory_space=pltpu.VMEM),
        scratch_shapes=[
            pltpu.VMEM((members * 8, part, channels), jnp.float32),
            pltpu.VMEM((members * 8, part, channels), jnp.bfloat16),
        ]
        + [pltpu.SemaphoreType.DMA((SUB, 8))] * 4,
        compiler_params=pltpu.CompilerParams(collective_id=0, has_side_effects=True, vmem_limit_bytes=32 << 20),
        name="score",
    )(forecast, truth)


def backward_kernel(cot_ref, w_hbm, hs_hbm, xs_hbm, slope_hbm, outa, outb, *scratch):
    (w, hs, xs, hsib, xsib, slope, cs, cp, csib, halo, ct, sa, ra, sb, rb, ta, tra, tb, trb) = scratch[:19]
    (um, uz, ur, v, vr, fin) = scratch[19:25]
    (local, sibs, sibr, hsend, hrecv, s1, r1, s2, r2, s3, r3, s4, r4, s5, r5) = scratch[25:]
    bf, f32 = jnp.bfloat16, jnp.float32
    member, rows = lax.axis_index("member"), lax.axis_index("rows")
    x, zh = member // 2, lax.rem(member, 2)
    y, z, c = rows // 8, lax.rem(rows // 2, 4), lax.rem(rows, 2)
    outs = (outa, outb)

    def at(px, pzh, py, pz, pc):
        return {"member": px * 2 + pzh, "rows": (py * 4 + pz) * 2 + pc}

    sibling = at(x, zh, y, z, 1 - c)
    far = at(x, 1 - zh, y, z, c)
    up = {"member": member, "rows": lax.rem(rows + 1, 32)}
    down = {"member": member, "rows": lax.rem(rows + 31, 32)}

    def along_y(k):
        return at(x, zh, lax.rem(y + k, 4), z, c)

    def along_x(k):
        return at(lax.rem(x + k, 4), zh, y, z, c)

    def cross_x(k):
        return at(lax.rem(x + k, 4), zh, y, z, 1 - c)

    def along_z(k):
        return at(x, zh, y, lax.rem(z + k, 4), c)

    def send(src, dst, ssem, rsem, to):
        return pltpu.make_async_remote_copy(
            src_ref=src, dst_ref=dst, send_sem=ssem, recv_sem=rsem, device_id=to, device_id_type=MESH
        )

    load_hs = pltpu.make_async_copy(hs_hbm, hs, local.at[0])
    load_w = pltpu.make_async_copy(w_hbm, w, local.at[1])
    load_slope = pltpu.make_async_copy(slope_hbm, slope, local.at[2])
    load_xs = pltpu.make_async_copy(xs_hbm, xs, local.at[3])
    load_hs.start()
    load_w.start()
    load_slope.start()
    load_xs.start()

    barrier = pltpu.get_barrier_semaphore()
    peers = [sibling, far, up, down]
    peers += [a(k) for a in (along_y, along_x, cross_x, along_z) for k in (1, 2, 3)]
    for p in peers:
        pl.semaphore_signal(barrier, inc=1, device_id=p, device_id_type=MESH)
    pl.semaphore_wait(barrier, len(peers))

    mine = pl.multiple_of(c * 256, 256)
    theirs = pl.multiple_of((1 - c) * 256, 256)
    to_up = send(cot_ref.at[pl.ds(384, 128)], halo.at[0], hsend.at[0], hrecv.at[0], up)
    to_down = send(cot_ref.at[pl.ds(0, 128)], halo.at[1], hsend.at[1], hrecv.at[1], down)
    cot_sib = send(cot_ref.at[:, pl.ds(theirs, 256)], csib.at[0], sibs.at[0], sibr.at[0], sibling)
    pre_sib = send(cp.at[:, pl.ds(theirs, 256)], csib.at[1], sibs.at[1], sibr.at[1], sibling)
    hs_sib = send(hs, hsib, sibs.at[2], sibr.at[2], sibling)
    xs_sib = send(xs, xsib, sibs.at[3], sibr.at[3], sibling)
    cot_sib.start()
    to_up.start()
    to_down.start()
    load_hs.wait()
    hs_sib.start()

    def shifted(block, place):
        wide = block.astype(f32)
        col = lax.broadcasted_iota(jnp.int32, wide.shape, 0)
        cs[0, pl.ds(place, 64)] = jnp.where(col == 0, 0.0, pltpu.roll(wide, 1, 0)).astype(bf)
        cs[1, pl.ds(place, 64)] = block
        cs[2, pl.ds(place, 64)] = jnp.where(col == 63, 0.0, pltpu.roll(wide, 63, 0)).astype(bf)

    @pl.loop(0, 8)
    def _(i):
        shifted(cot_ref[pl.ds(pl.multiple_of(i * 64, 64), 64)], pl.multiple_of(128 + i * 64, 64))

    def turned(value):
        return jnp.transpose(value.astype(f32), (1, 0)).astype(bf)

    def step1(g, grp, h, k):
        s, r = (sa, ra) if h == 0 else (sb, rb)
        to = lax.rem((y if h == 0 else x) + k, 4)
        return send(
            s.at[g, to, pl.ds(grp * 3, 3)],
            r.at[g, k - 1, pl.ds(grp * 3, 3)],
            s1.at[g, grp * 2 + h, k],
            r1.at[g, grp * 2 + h, k],
            along_y(k) if h == 0 else along_x(k),
        )

    def step2(g, h, k):
        s, r = (ta, tra) if h == 0 else (tb, trb)
        to = lax.rem((x if h == 0 else y) + k, 4)
        return send(
            s.at[g, to], r.at[g, k - 1], s2.at[g, h, k], r2.at[g, h, k], along_x(k) if h == 0 else along_y(k)
        )

    def step3(g, k):
        to = lax.rem(z + k, 4)
        return send(uz.at[g, to], ur.at[g, k - 1], s3.at[g, k], r3.at[g, k], along_z(k))

    def step4(g):
        return send(v.at[g], vr.at[g], s4.at[g], r4.at[g], far)

    spot = c * 4 + x

    def step5(g, k, cross):
        pc = (1 - c) if cross else c
        to = (cross_x(k) if k else sibling) if cross else along_x(k)
        i = k + 4 * cross
        return send(
            um.at[g, :, pl.ds(pl.multiple_of(pc * 16, 16), 16)],
            fin.at[g, spot],
            s5.at[g, i],
            r5.at[g, i],
            to,
        )

    every5 = [(k, 0) for k in (2, 1, 3)] + [(k, 1) for k in (2, 1, 3, 0)]

    def weight_gradient(g, own, sib):
        for grp in range(3):

            @pl.loop(0, 3)
            def _(b):
                total = jnp.dot(ct[0], own[b, grp * 128 : grp * 128 + 512], preferred_element_type=f32)
                total = total + jnp.dot(ct[1], sib[b, grp * 128 : grp * 128 + 512], preferred_element_type=f32)
                total = total.astype(bf)
                for xx in range(4):
                    for yy in range(4):
                        for h in range(2):
                            top = xx * 64 + h * 32
                            piece = total[top : top + 32, yy * 128 : yy * 128 + 128]
                            if h == 0:
                                sa[g, yy, grp * 3 + b, xx] = piece
                            else:
                                sb[g, xx, grp * 3 + b, yy] = piece

            for k in (2, 1, 3):
                step1(g, grp, 0, k).start()
                step1(g, grp, 1, k).start()

    ct[0] = turned(cot_ref[:, pl.ds(mine, 256)])
    cot_sib.wait_recv()
    ct[1] = turned(csib[0])
    hs_sib.wait_recv()
    weight_gradient(0, hs, hsib)

    load_xs.wait()
    xs_sib.start()
    to_up.wait_recv()
    to_down.wait_recv()
    for i in range(2):
        below, above = halo[0, i * 64 : i * 64 + 64], halo[1, i * 64 : i * 64 + 64]
        shifted(jnp.where(rows == 0, jnp.zeros_like(below), below), i * 64)
        shifted(jnp.where(rows == 31, jnp.zeros_like(above), above), 640 + i * 64)
    load_w.wait()
    load_slope.wait()

    for half in range(2):
        lanes = pl.ds(half * 256, 256)
        total = None
        for tap in range(9):
            view = cs[2 - tap % 3, pl.ds((2 - tap // 3) * 128, 512)]
            term = lax.dot_general(view, w[tap, lanes], (((1,), (1,)), ((), ())), preferred_element_type=f32)
            total = term if total is None else total + term
        cp[:, lanes] = (total * slope[:, lanes]).astype(bf)

    pre_sib.start()
    ct[0] = turned(cp[:, pl.ds(mine, 256)])
    pre_sib.wait_recv()
    ct[1] = turned(csib[1])
    xs_sib.wait_recv()
    weight_gradient(1, xs, xsib)

    def summed(own, got, where):
        total = own[where].astype(f32)
        for k in range(3):
            total = total + got[(k,) + where].astype(f32)
        return total

    um[...] = jnp.zeros_like(um)
    for g in range(2):
        for h in range(2):
            for grp in range(3):
                for k in (1, 2, 3):
                    step1(g, grp, h, k).wait_recv()
            own, got, into = ((sa, ra, ta), (sb, rb, tb))[h]
            here = y if h == 0 else x

            @pl.loop(0, 9)
            def _(tap):
                total = summed(own.at[g, here], got.at[g], (tap,)).astype(bf)
                for other in range(4):
                    into[g, other, tap] = total[other]

            for k in (2, 1, 3):
                step2(g, h, k).start()

        for h in range(2):
            for k in (1, 2, 3):
                step2(g, h, k).wait_recv()
        for pair in range(5):
            blocks = []
            for tap in (2 * pair, 2 * pair + 1):
                for h in range(2):
                    own, got = ((ta, tra), (tb, trb))[h]
                    here = x if h == 0 else y
                    blocks.append(
                        summed(own.at[g, here], got.at[g], (tap,)) if tap < 9 else jnp.zeros((32, 128), f32)
                    )
            flat = jnp.transpose(jnp.concatenate(blocks, axis=0), (1, 0)).astype(bf)
            for zz in range(4):
                uz[g, zz, pair] = flat[zz * 32 : zz * 32 + 32]
        for k in (2, 1, 3):
            step3(g, k).start()
        for k in (1, 2, 3):
            step3(g, k).wait_recv()
        v[g] = summed(uz.at[g, z], ur.at[g], (slice(None),)).astype(bf)
        step4(g).start()
        step4(g).wait_recv()
        um[g] = v[g].astype(f32) + vr[g].astype(f32)
        for k, cross in every5:
            step5(g, k, cross).start()
        fin[g, spot] = um[g, :, pl.ds(pl.multiple_of(c * 16, 16), 16)]

    for g in range(2):
        for k, cross in every5:
            step5(g, k, cross).wait_recv()
        for tap in range(9):
            off = (tap % 2) * 64
            row = [fin[g, i, tap // 2, :, off : off + 64] for i in range(8)]
            outs[g][tap] = jnp.concatenate(row, axis=1)

    to_up.wait_send()
    to_down.wait_send()
    for copy in (cot_sib, pre_sib, hs_sib, xs_sib):
        copy.wait_send()
    for g in range(2):
        step4(g).wait_send()
        for k in (1, 2, 3):
            for h in range(2):
                for grp in range(3):
                    step1(g, grp, h, k).wait_send()
                step2(g, h, k).wait_send()
            step3(g, k).wait_send()
        for k, cross in every5:
            step5(g, k, cross).wait_send()


def backward(cot, weight, hidden_shifts, state_shifts, slope):
    bf, f32 = jnp.bfloat16, jnp.float32
    dma = pltpu.SemaphoreType.DMA
    vmem = pltpu.VMEM
    pair = [vmem((2, 4, 9, 4, 32, 128), bf), vmem((2, 3, 9, 4, 32, 128), bf)]
    quad = [vmem((2, 4, 9, 32, 128), bf), vmem((2, 3, 9, 32, 128), bf)]
    scratch = [
        vmem((9, 512, 512), bf),
        vmem((3, 768, 512), bf),
        vmem((3, 768, 512), bf),
        vmem((3, 768, 512), bf),
        vmem((3, 768, 512), bf),
        vmem((512, 512), f32),
        vmem((3, 768, 512), bf),
        vmem((512, 512), bf),
        vmem((2, 512, 256), bf),
        vmem((2, 128, 512), bf),
        vmem((2, 256, 512), bf),
    ]
    scratch += pair + pair + quad + quad
    scratch += [
        vmem((2, 5, 32, 128), f32),
        vmem((2, 4, 5, 32, 128), bf),
        vmem((2, 3, 5, 32, 128), bf),
        vmem((2, 5, 32, 128), bf),
        vmem((2, 5, 32, 128), bf),
        vmem((2, 8, 5, 16, 128), f32),
    ]
    scratch += [dma((4,)), dma((4,)), dma((4,)), dma((2,)), dma((2,))]
    for dims in ((2, 6, 4), (2, 2, 4), (2, 4), (2,), (2, 8)):
        scratch += [dma(dims), dma(dims)]
    any_spec = pl.BlockSpec(memory_space=pl.ANY)
    outs = pl.pallas_call(
        backward_kernel,
        out_shape=[jax.ShapeDtypeStruct((9, 16, 512), f32)] * 2,
        in_specs=[pl.BlockSpec(memory_space=pltpu.VMEM)] + [any_spec] * 4,
        out_specs=[pl.BlockSpec(memory_space=pltpu.VMEM)] * 2,
        scratch_shapes=scratch,
        compiler_params=pltpu.CompilerParams(collective_id=1, has_side_effects=True, vmem_limit_bytes=56 << 20),
        name="backward",
    )(cot, weight, hidden_shifts, state_shifts, slope)
    return [jnp.transpose(o, (1, 0, 2)) for o in outs]


def body(state, truth, conv_first, conv_second):
    members, rows, cols, channels = state.shape
    state_pad = padded(state)
    pre = conv(state_pad, conv_first, rows, cols)
    hidden = gelu_value(pre).astype(jnp.bfloat16)
    hidden_pad = padded(hidden)
    forecast = state.astype(jnp.float32) + conv(hidden_pad, conv_second, rows, cols)
    prognosis = forecast.astype(jnp.bfloat16)
    cells = rows * cols
    cot = score(forecast.reshape(members, cells, channels), truth.reshape(cells, channels))
    cot = cot.reshape(members, rows, cols, channels)
    cot = jnp.transpose(cot, (1, 0, 2, 3)).reshape(-1, channels)
    slope = jnp.transpose(gelu_slope(pre), (1, 0, 2, 3)).reshape(-1, channels)
    second_slope, first_slope = backward(
        cot,
        jnp.transpose(conv_second, (1, 0, 2)),
        column_shifts(hidden_pad, cols),
        column_shifts(state_pad, cols),
        slope,
    )
    return prognosis, first_slope, second_slope


def solution(mesh):
    in_specs = (P("member", "rows", None, None), P("rows", None, None), P(), P())
    out_specs = (P("member", "rows", None, None), P("rows", None, None), P("rows", None, None))
    return jax.shard_map(body, mesh=mesh, in_specs=in_specs, out_specs=out_specs, check_vma=False)
```

```python
import functools

import jax
import jax.numpy as jnp
from jax import lax
from jax.experimental import pallas as pl
from jax.experimental.pallas import tpu as pltpu
from jax.sharding import PartitionSpec as P

MESH = pl.DeviceIdType.MESH
EPS2 = 0.1 * 0.1
INV_ROOT_TWO = 0.7071067811865476
INV_ROOT_TWOPI = 0.3989422804014327


def gelu_value(pre):
    return 0.5 * pre * (1.0 + lax.erf(pre * INV_ROOT_TWO))


def gelu_slope(pre):
    return 0.5 * (1.0 + lax.erf(pre * INV_ROOT_TWO)) + pre * jnp.exp(-0.5 * pre * pre) * INV_ROOT_TWOPI


def padded(field):
    count = lax.axis_size("rows")
    forward = [(i, i + 1) for i in range(count - 1)]
    backward = [(b, a) for a, b in forward]
    low = lax.ppermute(field[:, -1:], "rows", forward)
    high = lax.ppermute(field[:, :1], "rows", backward)
    field = jnp.concatenate([low, field, high], axis=1)
    return jnp.pad(field, ((0, 0), (0, 0), (1, 1), (0, 0)))


def tap_view(pad, tap, rows, cols):
    return pad[:, tap // 3 : tap // 3 + rows, tap % 3 : tap % 3 + cols, :].reshape(-1, pad.shape[3])


def conv(pad, kernel, rows, cols):
    total = 0.0
    for tap in range(9):
        total = total + jnp.dot(tap_view(pad, tap, rows, cols), kernel[:, tap, :], preferred_element_type=jnp.float32)
    return total.reshape(pad.shape[0], rows, cols, kernel.shape[2])


def column_shifts(pad, cols):
    ordered = jnp.transpose(pad, (1, 0, 2, 3))
    return jnp.stack([ordered[:, :, b : b + cols].reshape(-1, pad.shape[3]) for b in range(3)], axis=0)


SUB = 2


def score_kernel(f_ref, t_ref, out_ref, everyone, cots, s1, r1, s2, r2):
    member, rows = lax.axis_index("member"), lax.axis_index("rows")
    cells = everyone.shape[1]
    width = cells // SUB

    def peer(k):
        return {"member": lax.rem(member + k, 8), "rows": rows}

    barrier = pltpu.get_barrier_semaphore()
    for k in range(1, 8):
        pl.semaphore_signal(barrier, inc=1, device_id=peer(k), device_id_type=MESH)
    pl.semaphore_wait(barrier, 7)

    def out_copy(s, k):
        to = lax.rem(member + k, 8)
        start = pl.multiple_of(to * cells + s * width, 8)
        return pltpu.make_async_remote_copy(
            src_ref=f_ref.at[:, pl.ds(start, width)],
            dst_ref=everyone.at[pl.ds(member * 2, 2), pl.ds(s * width, width)],
            send_sem=s1.at[s, k],
            recv_sem=r1.at[s, k],
            device_id=peer(k),
            device_id_type=MESH,
        )

    def back_copy(s, k):
        to = lax.rem(member + k, 8)
        start = pl.multiple_of(member * cells + s * width, 8)
        return pltpu.make_async_remote_copy(
            src_ref=cots.at[pl.ds(to * 2, 2), pl.ds(s * width, width)],
            dst_ref=out_ref.at[:, pl.ds(start, width)],
            send_sem=s2.at[s, k],
            recv_sem=r2.at[s, k],
            device_id=peer(k),
            device_id_type=MESH,
        )

    for s in range(SUB):
        for k in (4, 3, 5, 1, 7, 2, 6):
            out_copy(s, k).start()
    mine = pl.multiple_of(member * cells, 8)
    everyone[pl.ds(member * 2, 2)] = f_ref[:, pl.ds(mine, cells)]
    for s in range(SUB):
        for k in range(1, 8):
            out_copy(s, k).wait_recv()

        @pl.loop(0, width // 16)
        def _(c):
            start = pl.multiple_of(s * width + c * 16, 16)
            tstart = pl.multiple_of(mine + s * width + c * 16, 16)
            for lane in range(0, 512, 128):
                spot = (pl.ds(start, 16), pl.ds(lane, 128))
                truth = t_ref[pl.ds(tstart, 16), pl.ds(lane, 128)].astype(jnp.float32)
                xs = [everyone[(k,) + spot] for k in range(16)]
                pulls = [None] * 16

                def plus(i, v):
                    pulls[i] = v if pulls[i] is None else pulls[i] + v

                for a in range(16):
                    for b in range(a + 1, 16):
                        d = xs[a] - xs[b]
                        u = d * lax.rsqrt(d * d + EPS2)
                        plus(a, u)
                        plus(b, -u)
                for k in range(16):
                    d = xs[k] - truth
                    slope = d * lax.rsqrt(d * d + EPS2)
                    cots[(k,) + spot] = (slope * (1.0 / 2048.0) - pulls[k] * (1.0 / 30720.0)).astype(jnp.bfloat16)

        for k in (4, 3, 5, 1, 7, 2, 6):
            back_copy(s, k).start()
    out_ref[:, pl.ds(mine, cells)] = cots[pl.ds(member * 2, 2)]
    for s in range(SUB):
        for k in range(1, 8):
            out_copy(s, k).wait_send()
            back_copy(s, k).wait()


def score(forecast, truth):
    members, cells, channels = forecast.shape
    part = cells // 8
    return pl.pallas_call(
        score_kernel,
        out_shape=jax.ShapeDtypeStruct(forecast.shape, jnp.bfloat16),
        in_specs=[pl.BlockSpec(memory_space=pltpu.VMEM)] * 2,
        out_specs=pl.BlockSpec(memory_space=pltpu.VMEM),
        scratch_shapes=[
            pltpu.VMEM((members * 8, part, channels), jnp.float32),
            pltpu.VMEM((members * 8, part, channels), jnp.bfloat16),
        ]
        + [pltpu.SemaphoreType.DMA((SUB, 8))] * 4,
        compiler_params=pltpu.CompilerParams(collective_id=0, has_side_effects=True, vmem_limit_bytes=32 << 20),
        name="score",
    )(forecast, truth)


SIZES = (4, 4, 1)


def backward_kernel(cot_ref, w_hbm, hs_hbm, xs_hbm, slope_hbm, outa, outb, *scratch):
    (w, hs, xs, hsib, xsib, slope, cs, cp, csib, halo, ct, sa, ra, sb, rb, ta, tra, tb, trb) = scratch[:19]
    (um, uz, ur, fin) = scratch[19:23]
    (local, sibs, sibr, hsend, hrecv, s1, r1, s2, r2, s3, r3, s5, r5) = scratch[23:]
    bf, f32 = jnp.bfloat16, jnp.float32
    member, rows = lax.axis_index("member"), lax.axis_index("rows")
    x, zh = member // 2, lax.rem(member, 2)
    y, z, c = rows // 8, lax.rem(rows // 2, 4), lax.rem(rows, 2)
    outs = (outa, outb)

    def at(px, pzh, py, pz, pc):
        return {"member": px * 2 + pzh, "rows": (py * 4 + pz) * 2 + pc}

    sibling = at(x, zh, y, z, 1 - c)
    up = {"member": member, "rows": lax.rem(rows + 1, 32)}
    down = {"member": member, "rows": lax.rem(rows + 31, 32)}

    def along_y(k):
        return at(x, zh, lax.rem(y + k, 4), z, c)

    def along_x(k):
        return at(lax.rem(x + k, 4), zh, y, z, c)

    def cross_x(k):
        return at(lax.rem(x + k, 4), zh, y, z, 1 - c)

    ring = zh * 4 + z

    def along_z(k):
        to = lax.rem(ring + k, 8)
        return at(x, to // 4, y, lax.rem(to, 4), c)

    def send(src, dst, ssem, rsem, to):
        return pltpu.make_async_remote_copy(
            src_ref=src, dst_ref=dst, send_sem=ssem, recv_sem=rsem, device_id=to, device_id_type=MESH
        )

    load_hs = pltpu.make_async_copy(hs_hbm, hs, local.at[0])
    load_w = pltpu.make_async_copy(w_hbm, w, local.at[1])
    load_slope = pltpu.make_async_copy(slope_hbm, slope, local.at[2])
    load_xs = pltpu.make_async_copy(xs_hbm, xs, local.at[3])
    load_hs.start()
    load_w.start()
    load_slope.start()
    load_xs.start()

    barrier = pltpu.get_barrier_semaphore()
    peers = [sibling, up, down] + [along_z(k) for k in range(1, 8)]
    peers += [a(k) for a in (along_y, along_x, cross_x) for k in (1, 2, 3)]
    for p in peers:
        pl.semaphore_signal(barrier, inc=1, device_id=p, device_id_type=MESH)
    pl.semaphore_wait(barrier, len(peers))

    mine = pl.multiple_of(c * 256, 256)
    theirs = pl.multiple_of((1 - c) * 256, 256)
    to_up = send(cot_ref.at[pl.ds(384, 128)], halo.at[0], hsend.at[0], hrecv.at[0], up)
    to_down = send(cot_ref.at[pl.ds(0, 128)], halo.at[1], hsend.at[1], hrecv.at[1], down)
    cot_sib = send(cot_ref.at[:, pl.ds(theirs, 256)], csib.at[0], sibs.at[0], sibr.at[0], sibling)
    pre_sib = send(cp.at[:, pl.ds(theirs, 256)], csib.at[1], sibs.at[1], sibr.at[1], sibling)
    hs_sib = send(hs, hsib, sibs.at[2], sibr.at[2], sibling)
    xs_sib = send(xs, xsib, sibs.at[3], sibr.at[3], sibling)
    cot_sib.start()
    to_up.start()
    to_down.start()
    load_hs.wait()
    hs_sib.start()

    def shifted(block, place):
        wide = block.astype(f32)
        col = lax.broadcasted_iota(jnp.int32, wide.shape, 0)
        cs[0, pl.ds(place, 64)] = jnp.where(col == 0, 0.0, pltpu.roll(wide, 1, 0)).astype(bf)
        cs[1, pl.ds(place, 64)] = block
        cs[2, pl.ds(place, 64)] = jnp.where(col == 63, 0.0, pltpu.roll(wide, 63, 0)).astype(bf)

    @pl.loop(0, 8)
    def _(i):
        shifted(cot_ref[pl.ds(pl.multiple_of(i * 64, 64), 64)], pl.multiple_of(128 + i * 64, 64))

    def turned(value):
        return jnp.transpose(value.astype(f32), (1, 0)).astype(bf)

    def step1(g, part, h, k):
        s, r = (sa, ra) if h == 0 else (sb, rb)
        to = lax.rem((y if h == 0 else x) + k, 4)
        taps = pl.ds(part * 4, SIZES[part])
        return send(
            s.at[g, to, taps],
            r.at[g, k - 1, taps],
            s1.at[g, part * 2 + h, k],
            r1.at[g, part * 2 + h, k],
            along_y(k) if h == 0 else along_x(k),
        )

    def step2(g, part, h, k):
        s, r = (ta, tra) if h == 0 else (tb, trb)
        to = lax.rem((x if h == 0 else y) + k, 4)
        taps = pl.ds(part * 4, SIZES[part])
        return send(
            s.at[g, to, taps],
            r.at[g, k - 1, taps],
            s2.at[g, part * 2 + h, k],
            r2.at[g, part * 2 + h, k],
            along_x(k) if h == 0 else along_y(k),
        )

    def step3(g, part, k):
        to = lax.rem(lax.rem(ring + k, 8), 4)
        pairs = pl.ds(part * 2, (SIZES[part] + 1) // 2)
        return send(uz.at[g, to, pairs], ur.at[g, ring, pairs], s3.at[g, part, k], r3.at[g, part, k], along_z(k))

    spot = c * 4 + x

    def step5(g, k, cross):
        pc = (1 - c) if cross else c
        to = (cross_x(k) if k else sibling) if cross else along_x(k)
        i = k + 4 * cross
        return send(um.at[g, pc], fin.at[g, spot], s5.at[g, i], r5.at[g, i], to)

    every5 = [(k, 0) for k in (2, 1, 3)] + [(k, 1) for k in (2, 1, 3, 0)]

    def form(g, part, own, sib):
        @pl.loop(part * 4, part * 4 + SIZES[part])
        def _(tap):
            b = lax.rem(tap, 3)
            view = pl.ds(pl.multiple_of((tap // 3) * 128, 128), 512)
            total = jnp.dot(ct[0], own[b, view], preferred_element_type=f32)
            total = total + jnp.dot(ct[1], sib[b, view], preferred_element_type=f32)
            total = total.astype(bf)
            for xx in range(4):
                for yy in range(4):
                    for h in range(2):
                        top = xx * 64 + h * 32
                        piece = total[top : top + 32, yy * 128 : yy * 128 + 128]
                        if h == 0:
                            sa[g, yy, tap, xx] = piece
                        else:
                            sb[g, xx, tap, yy] = piece

        for k in (2, 1, 3):
            step1(g, part, 0, k).start()
            step1(g, part, 1, k).start()

    def summed(own, got, where):
        total = own[where].astype(f32)
        for k in range(3):
            total = total + got[(k,) + where].astype(f32)
        return total

    def add1(g, part):
        for h in range(2):
            for k in (1, 2, 3):
                step1(g, part, h, k).wait_recv()
            own, got, into = ((sa, ra, ta), (sb, rb, tb))[h]
            here = y if h == 0 else x

            @pl.loop(part * 4, part * 4 + SIZES[part])
            def _(tap):
                total = summed(own.at[g, here], got.at[g], (tap,)).astype(bf)
                for other in range(4):
                    into[g, other, tap] = total[other]

            for k in (2, 1, 3):
                step2(g, part, h, k).start()

    def add2(g, part):
        for h in range(2):
            for k in (1, 2, 3):
                step2(g, part, h, k).wait_recv()
        for pair in range(part * 2, part * 2 + (SIZES[part] + 1) // 2):
            blocks = []
            for tap in (2 * pair, 2 * pair + 1):
                for h in range(2):
                    own, got = ((ta, tra), (tb, trb))[h]
                    here = x if h == 0 else y
                    blocks.append(
                        summed(own.at[g, here], got.at[g], (tap,)) if tap < 9 else jnp.zeros((32, 128), f32)
                    )
            flat = jnp.transpose(jnp.concatenate(blocks, axis=0), (1, 0)).astype(bf)
            for zz in range(4):
                uz[g, zz, pair] = flat[zz * 32 : zz * 32 + 32]
        for k in (4, 3, 5, 2, 6, 1, 7):
            step3(g, part, k).start()
        pairs = pl.ds(part * 2, (SIZES[part] + 1) // 2)
        ur[g, ring, pairs] = uz[g, z, pairs]

    def add3(g, part):
        for k in range(1, 8):
            step3(g, part, k).wait_recv()
        pairs = slice(part * 2, part * 2 + (SIZES[part] + 1) // 2)
        total = ur[g, 0, pairs].astype(f32)
        for q in range(1, 8):
            total = total + ur[g, q, pairs].astype(f32)
        total = total.astype(bf)
        um[g, 0, pairs] = total[:, :16]
        um[g, 1, pairs] = total[:, 16:]

    def spread(g):
        for k, cross in every5:
            step5(g, k, cross).start()
        fin[g, spot] = um[g, c]

    def finish(g):
        for k, cross in every5:
            step5(g, k, cross).wait_recv()
        for tap in range(9):
            off = (tap % 2) * 64
            row = [fin[g, i, tap // 2, :, off : off + 64].astype(f32) for i in range(8)]
            outs[g][tap] = jnp.concatenate(row, axis=1)

    ct[0] = turned(cot_ref[:, pl.ds(mine, 256)])
    cot_sib.wait_recv()
    ct[1] = turned(csib[0])
    hs_sib.wait_recv()
    for part in range(3):
        form(0, part, hs, hsib)

    load_xs.wait()
    xs_sib.start()
    to_up.wait_recv()
    to_down.wait_recv()
    for i in range(2):
        below, above = halo[0, i * 64 : i * 64 + 64], halo[1, i * 64 : i * 64 + 64]
        shifted(jnp.where(rows == 0, jnp.zeros_like(below), below), i * 64)
        shifted(jnp.where(rows == 31, jnp.zeros_like(above), above), 640 + i * 64)
    load_w.wait()
    load_slope.wait()

    for half in range(2):
        lanes = pl.ds(half * 256, 256)
        total = None
        for tap in range(9):
            view = cs[2 - tap % 3, pl.ds((2 - tap // 3) * 128, 512)]
            term = lax.dot_general(view, w[tap, lanes], (((1,), (1,)), ((), ())), preferred_element_type=f32)
            total = term if total is None else total + term
        cp[:, lanes] = (total * slope[:, lanes]).astype(bf)

    pre_sib.start()
    ct[0] = turned(cp[:, pl.ds(mine, 256)])
    pre_sib.wait_recv()
    ct[1] = turned(csib[1])
    xs_sib.wait_recv()
    add1(0, 0)
    form(1, 0, xs, xsib)
    add1(0, 1)
    form(1, 1, xs, xsib)
    add2(0, 0)
    form(1, 2, xs, xsib)
    add1(0, 2)
    add2(0, 1)
    add2(0, 2)
    add1(1, 0)
    add3(0, 0)
    add3(0, 1)
    add3(0, 2)
    spread(0)
    add2(1, 0)
    add1(1, 1)
    add1(1, 2)
    add2(1, 1)
    add2(1, 2)
    finish(0)
    add3(1, 0)
    add3(1, 1)
    add3(1, 2)
    spread(1)
    finish(1)

    to_up.wait_send()
    to_down.wait_send()
    for copy in (cot_sib, pre_sib, hs_sib, xs_sib):
        copy.wait_send()
    for g in range(2):
        for part in range(3):
            for k in (1, 2, 3):
                for h in range(2):
                    step1(g, part, h, k).wait_send()
                    step2(g, part, h, k).wait_send()
            for k in range(1, 8):
                step3(g, part, k).wait_send()
        for k, cross in every5:
            step5(g, k, cross).wait_send()


def backward(cot, weight, hidden_shifts, state_shifts, slope):
    bf, f32 = jnp.bfloat16, jnp.float32
    dma = pltpu.SemaphoreType.DMA
    vmem = pltpu.VMEM
    pair = [vmem((2, 4, 9, 4, 32, 128), bf), vmem((2, 3, 9, 4, 32, 128), bf)]
    quad = [vmem((2, 4, 9, 32, 128), bf), vmem((2, 3, 9, 32, 128), bf)]
    scratch = [
        vmem((9, 512, 512), bf),
        vmem((3, 768, 512), bf),
        vmem((3, 768, 512), bf),
        vmem((3, 768, 512), bf),
        vmem((3, 768, 512), bf),
        vmem((512, 512), f32),
        vmem((3, 768, 512), bf),
        vmem((512, 512), bf),
        vmem((2, 512, 256), bf),
        vmem((2, 128, 512), bf),
        vmem((2, 256, 512), bf),
    ]
    scratch += pair + pair + quad + quad
    scratch += [
        vmem((2, 2, 5, 16, 128), bf),
        vmem((2, 4, 5, 32, 128), bf),
        vmem((2, 8, 5, 32, 128), bf),
        vmem((2, 8, 5, 16, 128), bf),
    ]
    scratch += [dma((4,)), dma((4,)), dma((4,)), dma((2,)), dma((2,))]
    for dims in ((2, 6, 4), (2, 6, 4), (2, 3, 8), (2, 8)):
        scratch += [dma(dims), dma(dims)]
    any_spec = pl.BlockSpec(memory_space=pl.ANY)
    outs = pl.pallas_call(
        backward_kernel,
        out_shape=[jax.ShapeDtypeStruct((9, 16, 512), f32)] * 2,
        in_specs=[pl.BlockSpec(memory_space=pltpu.VMEM)] + [any_spec] * 4,
        out_specs=[pl.BlockSpec(memory_space=pltpu.VMEM)] * 2,
        scratch_shapes=scratch,
        compiler_params=pltpu.CompilerParams(collective_id=1, has_side_effects=True, vmem_limit_bytes=56 << 20),
        name="backward",
    )(cot, weight, hidden_shifts, state_shifts, slope)
    return [jnp.transpose(o, (1, 0, 2)) for o in outs]


def body(state, truth, conv_first, conv_second):
    members, rows, cols, channels = state.shape
    state_pad = padded(state)
    pre = conv(state_pad, conv_first, rows, cols)
    hidden = gelu_value(pre).astype(jnp.bfloat16)
    hidden_pad = padded(hidden)
    forecast = state.astype(jnp.float32) + conv(hidden_pad, conv_second, rows, cols)
    prognosis = forecast.astype(jnp.bfloat16)
    cells = rows * cols
    cot = score(forecast.reshape(members, cells, channels), truth.reshape(cells, channels))
    cot = cot.reshape(members, rows, cols, channels)
    cot = jnp.transpose(cot, (1, 0, 2, 3)).reshape(-1, channels)
    slope = jnp.transpose(gelu_slope(pre), (1, 0, 2, 3)).reshape(-1, channels)
    second_slope, first_slope = backward(
        cot,
        jnp.transpose(conv_second, (1, 0, 2)),
        column_shifts(hidden_pad, cols),
        column_shifts(state_pad, cols),
        slope,
    )
    return prognosis, first_slope, second_slope


def solution(mesh):
    in_specs = (P("member", "rows", None, None), P("rows", None, None), P(), P())
    out_specs = (P("member", "rows", None, None), P("rows", None, None), P("rows", None, None))
    return jax.shard_map(body, mesh=mesh, in_specs=in_specs, out_specs=out_specs, check_vma=False)
```

```python
import functools

import jax
import jax.numpy as jnp
from jax import lax
from jax.experimental import pallas as pl
from jax.experimental.pallas import tpu as pltpu
from jax.sharding import PartitionSpec as P

MESH = pl.DeviceIdType.MESH
EPS2 = 0.1 * 0.1
INV_ROOT_TWO = 0.7071067811865476
INV_ROOT_TWOPI = 0.3989422804014327


SIZES = (4, 4, 1)
AROUND = [(dr, dq) for dr in (-1, 0, 1) for dq in (-1, 0, 1) if dr or dq]


def step_kernel(spread_ref, truth_ref, w1_hbm, w2_hbm, prog_ref, outa, outb, *scratch):
    (w1, w2, stage, base, state, hidden, cots, state_sib, hidden_sib, slope, fore, leaving, cc, cp, csib) = scratch[:15]
    (ct, sa, ra, sb, rb, ta, tra, tb, trb, um, uz, ur, fin) = scratch[15:28]
    (local, sibs, sibr, hsend, hrecv, asend, arecv, s1, r1, s2, r2, s3, r3, s5, r5) = scratch[28:]
    bf, f32 = jnp.bfloat16, jnp.float32
    member, rows = lax.axis_index("member"), lax.axis_index("rows")
    x, zh = member // 2, lax.rem(member, 2)
    y, z, c = rows // 8, lax.rem(rows // 2, 4), lax.rem(rows, 2)
    q = zh * 4 + x
    outs = (outa, outb)

    def at(px, pzh, py, pz, pc):
        return {"member": px * 2 + pzh, "rows": (py * 4 + pz) * 2 + pc}

    def holder(pq):
        return lax.rem(pq, 4) * 2 + pq // 4

    sibling = at(x, zh, y, z, 1 - c)

    def mate(k):
        return {"member": holder(lax.rem(q + k, 8)), "rows": rows}

    def near(dr, dq):
        return {"member": holder(lax.rem(q + dq + 8, 8)), "rows": lax.rem(rows + dr + 32, 32)}

    def along_y(k):
        return at(x, zh, lax.rem(y + k, 4), z, c)

    def along_x(k):
        return at(lax.rem(x + k, 4), zh, y, z, c)

    def cross_x(k):
        return at(lax.rem(x + k, 4), zh, y, z, 1 - c)

    ring = zh * 4 + z

    def along_z(k):
        to = lax.rem(ring + k, 8)
        return at(x, to // 4, y, lax.rem(to, 4), c)

    def send(src, dst, ssem, rsem, to):
        return pltpu.make_async_remote_copy(
            src_ref=src, dst_ref=dst, send_sem=ssem, recv_sem=rsem, device_id=to, device_id_type=MESH
        )

    load_w1 = pltpu.make_async_copy(w1_hbm, w1, local.at[0])
    load_w2 = pltpu.make_async_copy(w2_hbm, w2, local.at[1])
    load_w1.start()
    load_w2.start()

    barrier = pltpu.get_barrier_semaphore()
    peers = [sibling] + [mate(k) for k in range(1, 8)] + [along_z(k) for k in range(1, 8)]
    peers += [near(dr, dq) for dr, dq in AROUND]
    peers += [a(k) for a in (along_y, along_x, cross_x) for k in (1, 2, 3)]
    for p in peers:
        pl.semaphore_signal(barrier, inc=1, device_id=p, device_id_type=MESH)
    pl.semaphore_wait(barrier, len(peers))

    def meet(k):
        to = lax.rem(q + k, 8)
        return send(spread_ref.at[to], stage.at[member], asend.at[0, k], arecv.at[0, k], mate(k))

    def leave(k):
        to = holder(lax.rem(q + k, 8))
        return send(leaving.at[to], prog_ref.at[q], asend.at[1, k], arecv.at[1, k], mate(k))

    far_first = (4, 3, 5, 2, 6, 1, 7)
    for k in far_first:
        meet(k).start()
    stage[member] = spread_ref[q]

    def halo(n, buf, i):
        dr, dq = AROUND[i]

        def cut(step, size, low, high):
            return pl.ds(low, size) if step == 0 else pl.ds(high if step > 0 else low, 1)

        def edge(step, size):
            return pl.ds(1, size) if step == 0 else pl.ds(0 if step > 0 else size + 1, 1)

        return send(
            buf.at[cut(dr, 4, 1, 4), cut(dq, 8, 1, 8)],
            buf.at[edge(dr, 4), edge(dq, 8)],
            hsend.at[n, i],
            hrecv.at[n, i],
            near(dr, dq),
        )

    def halo_start(n, buf):
        for i in range(8):
            halo(n, buf, i).start()

    def halo_wait(n, buf):
        for i in range(8):
            halo(n, buf, i).wait_recv()

        @pl.when(rows == 0)
        def _():
            buf[0] = jnp.zeros((10, 16, 512), bf)

        @pl.when(rows == 31)
        def _():
            buf[5] = jnp.zeros((10, 16, 512), bf)

        @pl.when(q == 0)
        def _():
            for r in range(6):
                buf[r, 0] = jnp.zeros((16, 512), bf)

        @pl.when(q == 7)
        def _():
            for r in range(6):
                buf[r, 9] = jnp.zeros((16, 512), bf)

    def view(buf, down, across):
        return buf[pl.ds(down, 4), pl.ds(across, 8)].reshape(512, 512)

    def turned(value):
        return jnp.transpose(value.astype(f32), (1, 0)).astype(bf)

    mine = pl.multiple_of(c * 256, 256)
    theirs = pl.multiple_of((1 - c) * 256, 256)
    state_out = send(state, state_sib, sibs.at[0], sibr.at[0], sibling)
    hidden_out = send(hidden, hidden_sib, sibs.at[1], sibr.at[1], sibling)
    cot_out = send(cc.at[:, pl.ds(theirs, 256)], csib.at[0], sibs.at[2], sibr.at[2], sibling)
    pre_out = send(cp.at[:, pl.ds(theirs, 256)], csib.at[1], sibs.at[3], sibr.at[3], sibling)

    def step1(g, part, h, k):
        s, r = (sa, ra) if h == 0 else (sb, rb)
        to = lax.rem((y if h == 0 else x) + k, 4)
        taps = pl.ds(part * 4, SIZES[part])
        return send(
            s.at[g, to, taps],
            r.at[g, k - 1, taps],
            s1.at[g, part * 2 + h, k],
            r1.at[g, part * 2 + h, k],
            along_y(k) if h == 0 else along_x(k),
        )

    def step2(g, part, h, k):
        s, r = (ta, tra) if h == 0 else (tb, trb)
        to = lax.rem((x if h == 0 else y) + k, 4)
        taps = pl.ds(part * 4, SIZES[part])
        return send(
            s.at[g, to, taps],
            r.at[g, k - 1, taps],
            s2.at[g, part * 2 + h, k],
            r2.at[g, part * 2 + h, k],
            along_x(k) if h == 0 else along_y(k),
        )

    def step3(g, part, k):
        to = lax.rem(lax.rem(ring + k, 8), 4)
        pairs = pl.ds(part * 2, (SIZES[part] + 1) // 2)
        return send(uz.at[g, to, pairs], ur.at[g, ring, pairs], s3.at[g, part, k], r3.at[g, part, k], along_z(k))

    spot = c * 4 + x

    def step5(g, k, cross):
        pc = (1 - c) if cross else c
        to = (cross_x(k) if k else sibling) if cross else along_x(k)
        i = k + 4 * cross
        return send(um.at[g, pc], fin.at[g, spot], s5.at[g, i], r5.at[g, i], to)

    every5 = [(k, 0) for k in (2, 1, 3)] + [(k, 1) for k in (2, 1, 3, 0)]

    def form(g, part, own, sib):
        @pl.loop(part * 4, part * 4 + SIZES[part])
        def _(tap):
            down, across = tap // 3, lax.rem(tap, 3)
            total = jnp.dot(ct[0], view(own, down, across), preferred_element_type=f32)
            total = total + jnp.dot(ct[1], view(sib, down, across), preferred_element_type=f32)
            total = total.astype(bf)
            for xx in range(4):
                for yy in range(4):
                    for h in range(2):
                        top = xx * 64 + h * 32
                        piece = total[top : top + 32, yy * 128 : yy * 128 + 128]
                        if h == 0:
                            sa[g, yy, tap, xx] = piece
                        else:
                            sb[g, xx, tap, yy] = piece

        for k in (2, 1, 3):
            step1(g, part, 0, k).start()
            step1(g, part, 1, k).start()

    def summed(own, got, where):
        total = own[where].astype(f32)
        for k in range(3):
            total = total + got[(k,) + where].astype(f32)
        return total

    def add1(g, part):
        for h in range(2):
            for k in (1, 2, 3):
                step1(g, part, h, k).wait_recv()
            own, got, into = ((sa, ra, ta), (sb, rb, tb))[h]
            here = y if h == 0 else x

            @pl.loop(part * 4, part * 4 + SIZES[part])
            def _(tap):
                total = summed(own.at[g, here], got.at[g], (tap,)).astype(bf)
                for other in range(4):
                    into[g, other, tap] = total[other]

            for k in (2, 1, 3):
                step2(g, part, h, k).start()

    def add2(g, part):
        for h in range(2):
            for k in (1, 2, 3):
                step2(g, part, h, k).wait_recv()
        for pair in range(part * 2, part * 2 + (SIZES[part] + 1) // 2):
            blocks = []
            for tap in (2 * pair, 2 * pair + 1):
                for h in range(2):
                    own, got = ((ta, tra), (tb, trb))[h]
                    here = x if h == 0 else y
                    blocks.append(
                        summed(own.at[g, here], got.at[g], (tap,)) if tap < 9 else jnp.zeros((32, 128), f32)
                    )
            flat = jnp.transpose(jnp.concatenate(blocks, axis=0), (1, 0)).astype(bf)
            for zz in range(4):
                uz[g, zz, pair] = flat[zz * 32 : zz * 32 + 32]
        for k in (4, 3, 5, 2, 6, 1, 7):
            step3(g, part, k).start()
        pairs = pl.ds(part * 2, (SIZES[part] + 1) // 2)
        ur[g, ring, pairs] = uz[g, z, pairs]

    def add3(g, part):
        for k in range(1, 8):
            step3(g, part, k).wait_recv()
        pairs = slice(part * 2, part * 2 + (SIZES[part] + 1) // 2)
        total = ur[g, 0, pairs].astype(f32)
        for q in range(1, 8):
            total = total + ur[g, q, pairs].astype(f32)
        total = total.astype(bf)
        um[g, 0, pairs] = total[:, :16]
        um[g, 1, pairs] = total[:, 16:]

    def spread(g):
        for k, cross in every5:
            step5(g, k, cross).start()
        fin[g, spot] = um[g, c]

    def finish(g):
        for k, cross in every5:
            step5(g, k, cross).wait_recv()
        for tap in range(9):
            off = (tap % 2) * 64
            row = [fin[g, i, tap // 2, :, off : off + 64].astype(f32) for i in range(8)]
            outs[g][tap] = jnp.concatenate(row, axis=1)

    for k in range(1, 8):
        meet(k).wait_recv()

    @pl.loop(0, 8)
    def _(m):
        for j in range(2):
            for l in range(4):
                lanes = slice(l * 128, l * 128 + 128)
                value = stage[m, j * 32 : j * 32 + 32, lanes].astype(f32)
                base[l, pl.ds(m * 2 + j, 32, stride=16), :] = value

    for l in range(4):
        state[1:5, 1:9, :, l * 128 : l * 128 + 128] = base[l].astype(bf).reshape(4, 8, 16, 128)
    halo_start(0, state)
    load_w1.wait()
    halo_wait(0, state)
    state_out.start()

    def conv(buf, w, half):
        total = None
        for tap in range(9):
            term = jnp.dot(
                view(buf, tap // 3, tap % 3), w[tap, :, half * 256 : half * 256 + 256], preferred_element_type=f32
            )
            total = term if total is None else total + term
        return total

    for half in range(2):
        lanes = slice(half * 256, half * 256 + 256)
        pre = conv(state, w1, half)
        both = 0.5 * (1.0 + lax.erf(pre * INV_ROOT_TWO))
        slope[:, lanes] = both + pre * jnp.exp(-0.5 * pre * pre) * INV_ROOT_TWOPI
        hidden[1:5, 1:9, :, lanes] = (pre * both).astype(bf).reshape(4, 8, 16, 256)

    halo_start(1, hidden)
    load_w2.wait()
    halo_wait(1, hidden)
    hidden_out.start()
    for half in range(2):
        total = conv(hidden, w2, half)
        for l in range(2):
            fore[half * 2 + l] = base[half * 2 + l] + total[:, l * 128 : l * 128 + 128]

    for l in range(4):
        for k in range(16):
            value = fore[l, pl.ds(k, 32, stride=16), :]
            leaving[k // 2, (k % 2) * 32 : (k % 2) * 32 + 32, l * 128 : l * 128 + 128] = value.astype(bf)

    @pl.loop(0, 4)
    def _(l):
        @pl.loop(0, 4)
        def _(cell):
            truth = truth_ref[q, l, pl.ds(pl.multiple_of(cell * 8, 8), 8), :]

            def spot_of(k):
                return pl.ds(cell * 128 + k, 8, stride=16)

            xs = [fore[l, spot_of(k), :] for k in range(16)]
            pulls = [None] * 16

            def plus(i, v):
                pulls[i] = v if pulls[i] is None else pulls[i] + v

            for a in range(16):
                for b in range(a + 1, 16):
                    d = xs[a] - xs[b]
                    u = d * lax.rsqrt(d * d + EPS2)
                    plus(a, u)
                    plus(b, -u)
            for k in range(16):
                d = xs[k] - truth
                away = d * lax.rsqrt(d * d + EPS2)
                fore[l, spot_of(k), :] = away * (1.0 / 2048.0) - pulls[k] * (1.0 / 30720.0)

    for l in range(4):
        lanes = slice(l * 128, l * 128 + 128)
        value = fore[l].astype(bf)
        cc[:, lanes] = value
        cots[1:5, 1:9, :, lanes] = value.reshape(4, 8, 16, 128)
    cot_out.start()
    halo_start(2, cots)
    for k in far_first:
        leave(k).start()
    prog_ref[q] = leaving[member]

    ct[0] = turned(cc[:, pl.ds(mine, 256)])
    cot_out.wait_recv()
    ct[1] = turned(csib[0])
    hidden_out.wait_recv()
    for part in range(3):
        form(0, part, hidden, hidden_sib)

    halo_wait(2, cots)
    for half in range(2):
        lanes = pl.ds(half * 256, 256)
        total = None
        for tap in range(9):
            term = lax.dot_general(
                view(cots, 2 - tap // 3, 2 - tap % 3),
                w2[tap, lanes],
                (((1,), (1,)), ((), ())),
                preferred_element_type=f32,
            )
            total = term if total is None else total + term
        cp[:, lanes] = (total * slope[:, lanes]).astype(bf)

    pre_out.start()
    ct[0] = turned(cp[:, pl.ds(mine, 256)])
    pre_out.wait_recv()
    ct[1] = turned(csib[1])
    state_out.wait_recv()
    add1(0, 0)
    form(1, 0, state, state_sib)
    add1(0, 1)
    form(1, 1, state, state_sib)
    add2(0, 0)
    form(1, 2, state, state_sib)
    add1(0, 2)
    add2(0, 1)
    add2(0, 2)
    add1(1, 0)
    add3(0, 0)
    add3(0, 1)
    add3(0, 2)
    spread(0)
    add2(1, 0)
    add1(1, 1)
    add1(1, 2)
    add2(1, 1)
    add2(1, 2)
    finish(0)
    add3(1, 0)
    add3(1, 1)
    add3(1, 2)
    spread(1)
    finish(1)

    for k in range(1, 8):
        meet(k).wait_send()
        leave(k).wait()
    for copy in (state_out, hidden_out, cot_out, pre_out):
        copy.wait_send()
    for n, buf in enumerate((state, hidden, cots)):
        for i in range(8):
            halo(n, buf, i).wait_send()
    for g in range(2):
        for part in range(3):
            for k in (1, 2, 3):
                for h in range(2):
                    step1(g, part, h, k).wait_send()
                    step2(g, part, h, k).wait_send()
            for k in range(1, 8):
                step3(g, part, k).wait_send()
        for k, cross in every5:
            step5(g, k, cross).wait_send()


def whole_step(spread, truth, first, second):
    bf, f32 = jnp.bfloat16, jnp.float32
    dma = pltpu.SemaphoreType.DMA
    vmem = pltpu.VMEM
    pair = [vmem((2, 4, 9, 4, 32, 128), bf), vmem((2, 3, 9, 4, 32, 128), bf)]
    quad = [vmem((2, 4, 9, 32, 128), bf), vmem((2, 3, 9, 32, 128), bf)]
    block = vmem((6, 10, 16, 512), bf)
    scratch = [
        vmem((9, 512, 512), bf),
        vmem((9, 512, 512), bf),
        vmem((8, 64, 512), bf),
        vmem((4, 512, 128), f32),
        block,
        block,
        block,
        block,
        block,
        vmem((512, 512), f32),
        vmem((4, 512, 128), f32),
        vmem((8, 64, 512), bf),
        vmem((512, 512), bf),
        vmem((512, 512), bf),
        vmem((2, 512, 256), bf),
        vmem((2, 256, 512), bf),
    ]
    scratch += pair + pair + quad + quad
    scratch += [
        vmem((2, 2, 5, 16, 128), bf),
        vmem((2, 4, 5, 32, 128), bf),
        vmem((2, 8, 5, 32, 128), bf),
        vmem((2, 8, 5, 16, 128), bf),
    ]
    scratch += [dma((2,)), dma((4,)), dma((4,)), dma((3, 8)), dma((3, 8)), dma((2, 8)), dma((2, 8))]
    for dims in ((2, 6, 4), (2, 6, 4), (2, 3, 8), (2, 8)):
        scratch += [dma(dims), dma(dims)]
    in_vmem = pl.BlockSpec(memory_space=pltpu.VMEM)
    return pl.pallas_call(
        step_kernel,
        out_shape=[jax.ShapeDtypeStruct((8, 64, 512), bf)] + [jax.ShapeDtypeStruct((9, 16, 512), f32)] * 2,
        in_specs=[in_vmem] * 2 + [pl.BlockSpec(memory_space=pl.ANY)] * 2,
        out_specs=[in_vmem] * 3,
        scratch_shapes=scratch,
        compiler_params=pltpu.CompilerParams(collective_id=0, has_side_effects=True, vmem_limit_bytes=60 << 20),
        name="whole_step",
    )(spread, truth, first, second)


def body(state, truth, conv_first, conv_second):
    members, rows, cols, channels = state.shape
    width = cols // 8
    spread = state.reshape(members, rows, 8, width, channels).transpose(2, 0, 1, 3, 4)
    facts = truth.astype(jnp.float32).reshape(rows, 8, width, channels // 128, 128).transpose(1, 3, 0, 2, 4)
    prognosis, second_slope, first_slope = whole_step(
        spread.reshape(8, members * rows * width, channels),
        facts.reshape(8, channels // 128, rows * width, 128),
        jnp.transpose(conv_first, (1, 0, 2)),
        jnp.transpose(conv_second, (1, 0, 2)),
    )
    prognosis = prognosis.reshape(8, members, rows, width, channels).transpose(1, 2, 0, 3, 4).reshape(state.shape)
    return prognosis, jnp.transpose(first_slope, (1, 0, 2)), jnp.transpose(second_slope, (1, 0, 2))


def solution(mesh):
    in_specs = (P("member", "rows", None, None), P("rows", None, None), P(), P())
    out_specs = (P("member", "rows", None, None), P("rows", None, None), P("rows", None, None))
    return jax.shard_map(body, mesh=mesh, in_specs=in_specs, out_specs=out_specs, check_vma=False)
```

```python
import functools

import jax
import jax.numpy as jnp
from jax import lax
from jax.experimental import pallas as pl
from jax.experimental.pallas import tpu as pltpu
from jax.sharding import PartitionSpec as P

MESH = pl.DeviceIdType.MESH
EPS2 = 0.1 * 0.1
INV_ROOT_TWO = 0.7071067811865476
INV_ROOT_TWOPI = 0.3989422804014327


SIZES = (4, 4, 1)
WIDE = 40
HEIGHT = (WIDE, 64 - WIDE)
AROUND = [(dr, dq) for dr in (-1, 0, 1) for dq in (-1, 0, 1) if dr or dq]


def step_kernel(state_hbm, truth_hbm, w1_hbm, w2_hbm, prog_ref, out_ref, *scratch):
    (w1, w2, stage, base, state, hidden, cots, state_sib, hidden_sib, slope, fore, leaving, cc, cp, csib, truth) = scratch[:16]
    (ct, sa, ra, sb, rb, ta, tra, tb, trb, um, uz, ur, fin) = scratch[16:29]
    (local, sibs, sibr, hsend, hrecv, asend, arecv, s1, r1, s2, r2, s3, r3, s5, r5) = scratch[29:]
    bf, f32 = jnp.bfloat16, jnp.float32
    member, rows = lax.axis_index("member"), lax.axis_index("rows")
    x, zh = member // 2, lax.rem(member, 2)
    y, z, c = rows // 8, lax.rem(rows // 2, 4), lax.rem(rows, 2)
    q = zh * 4 + x

    def at(px, pzh, py, pz, pc):
        return {"member": px * 2 + pzh, "rows": (py * 4 + pz) * 2 + pc}

    def holder(pq):
        return lax.rem(pq, 4) * 2 + pq // 4

    sibling = at(x, zh, y, z, 1 - c)

    def mate(k):
        return {"member": holder(lax.rem(q + k, 8)), "rows": rows}

    def near(dr, dq):
        return {"member": holder(lax.rem(q + dq + 8, 8)), "rows": lax.rem(rows + dr + 32, 32)}

    def along_y(k):
        return at(x, zh, lax.rem(y + k, 4), z, c)

    def along_x(k):
        return at(lax.rem(x + k, 4), zh, y, z, c)

    def cross_x(k):
        return at(lax.rem(x + k, 4), zh, y, z, 1 - c)

    ring = zh * 4 + z

    def along_z(k):
        to = lax.rem(ring + k, 8)
        return at(x, to // 4, y, lax.rem(to, 4), c)

    def send(src, dst, ssem, rsem, to):
        return pltpu.make_async_remote_copy(
            src_ref=src, dst_ref=dst, send_sem=ssem, recv_sem=rsem, device_id=to, device_id_type=MESH
        )

    load_w1 = pltpu.make_async_copy(w1_hbm, w1, local.at[0])
    load_w2 = pltpu.make_async_copy(w2_hbm, w2, local.at[1])
    load_w1.start()
    load_w2.start()

    barrier = pltpu.get_barrier_semaphore()
    peers = [mate(k) for k in range(1, 8)] + [along_z(k) for k in (1, 2, 3, 5, 6, 7)]
    peers += [near(dr, dq) for dr, dq in AROUND if dr]
    peers += [a(k) for a in (along_y, cross_x) for k in (1, 2, 3)]
    for p in peers:
        pl.semaphore_signal(barrier, inc=1, device_id=p, device_id_type=MESH)
    pl.semaphore_wait(barrier, len(peers))

    def columns(pq):
        return pl.ds(pl.multiple_of(pq * 8, 8), 8)

    own_state = pltpu.make_async_copy(state_hbm.at[:, :, columns(q)], stage.at[member], local.at[2])
    own_truth = pltpu.make_async_copy(truth_hbm.at[:, columns(q)], truth, local.at[3])

    def meet(k):
        to = lax.rem(q + k, 8)
        return send(state_hbm.at[:, :, columns(to)], stage.at[member], asend.at[0, k], arecv.at[0, k], mate(k))

    def leave(k):
        to = holder(lax.rem(q + k, 8))
        return send(leaving.at[to], prog_ref.at[q], asend.at[1, k], arecv.at[1, k], mate(k))

    far_first = (4, 3, 5, 2, 6, 1, 7)
    for k in far_first:
        meet(k).start()
    own_state.start()
    own_truth.start()

    def halo(n, buf, i):
        dr, dq = AROUND[i]

        def cut(step, size, low, high):
            return pl.ds(low, size) if step == 0 else pl.ds(high if step > 0 else low, 1)

        def edge(step, size):
            return pl.ds(1, size) if step == 0 else pl.ds(0 if step > 0 else size + 1, 1)

        return send(
            buf.at[cut(dr, 4, 1, 4), cut(dq, 8, 1, 8)],
            buf.at[edge(dr, 4), edge(dq, 8)],
            hsend.at[n, i],
            hrecv.at[n, i],
            near(dr, dq),
        )

    def inside(dr, dq):
        there = None
        for ok in [rows > 0] * (dr < 0) + [rows < 31] * (dr > 0) + [q > 0] * (dq < 0) + [q < 7] * (dq > 0):
            there = ok if there is None else jnp.logical_and(there, ok)
        return there

    def halo_start(n, buf):
        for i, (dr, dq) in enumerate(AROUND):
            @pl.when(inside(dr, dq))
            def _():
                halo(n, buf, i).start()

    def halo_sent(n, buf):
        for i, (dr, dq) in enumerate(AROUND):
            @pl.when(inside(dr, dq))
            def _():
                halo(n, buf, i).wait_send()

    def halo_wait(n, buf):
        for i, (dr, dq) in enumerate(AROUND):
            @pl.when(inside(-dr, -dq))
            def _():
                halo(n, buf, i).wait_recv()

        @pl.when(rows == 0)
        def _():
            buf[0] = jnp.zeros((10, 16, 512), bf)

        @pl.when(rows == 31)
        def _():
            buf[5] = jnp.zeros((10, 16, 512), bf)

        @pl.when(q == 0)
        def _():
            for r in range(6):
                buf[r, 0] = jnp.zeros((16, 512), bf)

        @pl.when(q == 7)
        def _():
            for r in range(6):
                buf[r, 9] = jnp.zeros((16, 512), bf)

    def view(buf, down, across):
        return buf[pl.ds(down, 4), pl.ds(across, 8)].reshape(512, 512)

    def turned(value):
        return jnp.transpose(value.astype(f32), (1, 0)).astype(bf)

    mine = pl.multiple_of(c * 256, 256)
    theirs = pl.multiple_of((1 - c) * 256, 256)
    state_out = send(state, state_sib, sibs.at[0], sibr.at[0], sibling)
    hidden_out = send(hidden, hidden_sib, sibs.at[1], sibr.at[1], sibling)
    cot_out = send(cc.at[:, pl.ds(theirs, 256)], csib.at[0], sibs.at[2], sibr.at[2], sibling)
    pre_out = send(cp.at[:, pl.ds(theirs, 256)], csib.at[1], sibs.at[3], sibr.at[3], sibling)

    def step1(g, part, h, k):
        s, r = (sa, ra) if h == 0 else (sb, rb)
        to = lax.rem((y if h == 0 else x) + k, 4)
        taps = pl.ds(part * 4, SIZES[part])
        return send(
            s.at[g, to, taps],
            r.at[g, k - 1, taps],
            s1.at[g, part * 2 + h, k],
            r1.at[g, part * 2 + h, k],
            along_y(k) if h == 0 else along_x(k),
        )

    def step2(g, part, h, k):
        s, r = (ta, tra) if h == 0 else (tb, trb)
        to = lax.rem((x if h == 0 else y) + k, 4)
        taps = pl.ds(part * 4, SIZES[part])
        return send(
            s.at[g, to, taps],
            r.at[g, k - 1, taps],
            s2.at[g, part * 2 + h, k],
            r2.at[g, part * 2 + h, k],
            along_x(k) if h == 0 else along_y(k),
        )

    def step3(g, part, k):
        to = lax.rem(lax.rem(ring + k, 8), 4)
        pairs = pl.ds(part * 2, (SIZES[part] + 1) // 2)
        return send(uz.at[g, to, pairs], ur.at[g, ring, pairs], s3.at[g, part, k], r3.at[g, part, k], along_z(k))

    spot = c * 4 + x

    def step5(g, k, cross):
        pc = (1 - c) if cross else c
        to = (cross_x(k) if k else sibling) if cross else along_x(k)
        i = k + 4 * cross
        return send(um.at[g, pc], fin.at[g, spot], s5.at[g, i], r5.at[g, i], to)

    every5 = [(k, 0) for k in (2, 1, 3)] + [(k, 1) for k in (2, 1, 3, 0)]

    def form(g, part, own, sib):
        @pl.loop(part * 4, part * 4 + SIZES[part])
        def _(tap):
            down, across = tap // 3, lax.rem(tap, 3)
            total = jnp.dot(ct[0], view(own, down, across), preferred_element_type=f32)
            total = total + jnp.dot(ct[1], view(sib, down, across), preferred_element_type=f32)
            for xx in range(4):
                for yy in range(4):
                    for h in range(2):
                        top = xx * 64 + h * WIDE
                        piece = total[top : top + HEIGHT[h], yy * 128 : yy * 128 + 128].astype(bf)
                        if h == 0:
                            sa[g, yy, tap, xx] = piece
                        else:
                            sb[g, xx, tap, yy] = piece

        for k in (2, 1, 3):
            step1(g, part, 0, k).start()
            step1(g, part, 1, k).start()

    def summed(own, got, where):
        total = own[where].astype(f32)
        for k in range(3):
            total = total + got[(k,) + where].astype(f32)
        return total

    def add1(g, part):
        for h in range(2):
            for k in (1, 2, 3):
                step1(g, part, h, k).wait_recv()
            own, got, into = ((sa, ra, ta), (sb, rb, tb))[h]
            here = y if h == 0 else x

            @pl.loop(part * 4, part * 4 + SIZES[part])
            def _(tap):
                total = summed(own.at[g, here], got.at[g], (tap,)).astype(bf)
                for other in range(4):
                    into[g, other, tap] = total[other]

            for k in (2, 1, 3):
                step2(g, part, h, k).start()

    def add2(g, part):
        for h in range(2):
            for k in (1, 2, 3):
                step2(g, part, h, k).wait_recv()
        for pair in range(part * 2, part * 2 + (SIZES[part] + 1) // 2):
            blocks = []
            for tap in (2 * pair, 2 * pair + 1):
                for h in range(2):
                    own, got = ((ta, tra), (tb, trb))[h]
                    here = x if h == 0 else y
                    blocks.append(
                        summed(own.at[g, here], got.at[g], (tap,)) if tap < 9 else jnp.zeros((HEIGHT[h], 128), f32)
                    )
            flat = jnp.transpose(jnp.concatenate(blocks, axis=0), (1, 0)).astype(bf)
            for zz in range(4):
                uz[g, zz, pair] = flat[zz * 32 : zz * 32 + 32]
        for k in (4, 3, 5, 2, 6, 1, 7):
            step3(g, part, k).start()
        pairs = pl.ds(part * 2, (SIZES[part] + 1) // 2)
        ur[g, ring, pairs] = uz[g, z, pairs]

    def add3(g, part):
        for k in range(1, 8):
            step3(g, part, k).wait_recv()
        pairs = slice(part * 2, part * 2 + (SIZES[part] + 1) // 2)
        total = ur[g, 0, pairs].astype(f32)
        for q in range(1, 8):
            total = total + ur[g, q, pairs].astype(f32)
        total = total.astype(bf)
        um[g, 0, pairs] = total[:, :16]
        um[g, 1, pairs] = total[:, 16:]

    def spread(g):
        for k, cross in every5:
            step5(g, k, cross).start()
        fin[g, spot] = um[g, c]

    def finish(g):
        for k, cross in every5:
            step5(g, k, cross).wait_recv()
        for tap in range(9):
            off = (tap % 2) * 64
            row = [fin[g, i, tap // 2, :, off : off + 64] for i in range(8)]
            out_ref[g, tap] = jnp.concatenate(row, axis=1)

    own_state.wait()
    for k in range(1, 8):
        meet(k).wait_recv()

    @pl.loop(0, 8)
    def _(m):
        for j in range(2):
            for l in range(4):
                lanes = slice(l * 128, l * 128 + 128)
                value = stage[m, j, :, :, lanes].astype(f32).reshape(32, 128)
                base[l, pl.ds(m * 2 + j, 32, stride=16), :] = value

    for l in range(4):
        state[1:5, 1:9, :, l * 128 : l * 128 + 128] = base[l].astype(bf).reshape(4, 8, 16, 128)
    halo_start(0, state)
    load_w1.wait()
    halo_wait(0, state)
    state_out.start()

    def conv(buf, w, half):
        total = None
        for tap in range(9):
            term = jnp.dot(
                view(buf, tap // 3, tap % 3), w[tap, :, half * 256 : half * 256 + 256], preferred_element_type=f32
            )
            total = term if total is None else total + term
        return total

    for half in range(2):
        lanes = slice(half * 256, half * 256 + 256)
        pre = conv(state, w1, half)
        both = 0.5 * (1.0 + lax.erf(pre * INV_ROOT_TWO))
        slope[:, lanes] = both + pre * jnp.exp(-0.5 * pre * pre) * INV_ROOT_TWOPI
        hidden[1:5, 1:9, :, lanes] = (pre * both).astype(bf).reshape(4, 8, 16, 256)

    halo_start(1, hidden)
    load_w2.wait()
    halo_wait(1, hidden)
    hidden_out.start()
    for half in range(2):
        total = conv(hidden, w2, half)
        for l in range(2):
            fore[half * 2 + l] = base[half * 2 + l] + total[:, l * 128 : l * 128 + 128]

    for l in range(4):
        for k in range(16):
            value = fore[l, pl.ds(k, 32, stride=16), :]
            leaving[k // 2, (k % 2) * 32 : (k % 2) * 32 + 32, l * 128 : l * 128 + 128] = value.astype(bf)

    own_truth.wait()

    @pl.loop(0, 4)
    def _(l):
        @pl.loop(0, 4)
        def _(cell):
            fact = truth[cell, :, pl.ds(pl.multiple_of(l * 128, 128), 128)].astype(f32)

            def spot_of(k):
                return pl.ds(cell * 128 + k, 8, stride=16)

            xs = [fore[l, spot_of(k), :] for k in range(16)]
            pulls = [None] * 16

            def plus(i, v):
                pulls[i] = v if pulls[i] is None else pulls[i] + v

            for a in range(16):
                for b in range(a + 1, 16):
                    d = xs[a] - xs[b]
                    u = d * lax.rsqrt(d * d + EPS2)
                    plus(a, u)
                    plus(b, -u)
            for k in range(16):
                d = xs[k] - fact
                away = d * lax.rsqrt(d * d + EPS2)
                fore[l, spot_of(k), :] = away * (1.0 / 2048.0) - pulls[k] * (1.0 / 30720.0)

    for l in range(4):
        lanes = slice(l * 128, l * 128 + 128)
        value = fore[l].astype(bf)
        cc[:, lanes] = value
        cots[1:5, 1:9, :, lanes] = value.reshape(4, 8, 16, 128)
    cot_out.start()
    halo_start(2, cots)

    ct[0] = turned(cc[:, pl.ds(mine, 256)])
    cot_out.wait_recv()
    ct[1] = turned(csib[0])
    hidden_out.wait_recv()
    for part in range(3):
        form(0, part, hidden, hidden_sib)

    halo_wait(2, cots)
    for k in far_first:
        leave(k).start()
    prog_ref[q] = leaving[member]
    for half in range(2):
        lanes = pl.ds(half * 256, 256)
        total = None
        for tap in range(9):
            term = lax.dot_general(
                view(cots, 2 - tap // 3, 2 - tap % 3),
                w2[tap, lanes],
                (((1,), (1,)), ((), ())),
                preferred_element_type=f32,
            )
            total = term if total is None else total + term
        cp[:, lanes] = (total * slope[:, lanes]).astype(bf)

    pre_out.start()
    ct[0] = turned(cp[:, pl.ds(mine, 256)])
    pre_out.wait_recv()
    ct[1] = turned(csib[1])
    state_out.wait_recv()
    for part in range(3):
        add1(0, part)
    for part in range(3):
        form(1, part, state, state_sib)
    for part in range(3):
        add2(0, part)
    for part in range(3):
        add3(0, part)
    spread(0)
    for part in range(3):
        add1(1, part)
    for part in range(3):
        add2(1, part)
    finish(0)
    for part in range(3):
        add3(1, part)
    spread(1)
    finish(1)

    for k in range(1, 8):
        meet(k).wait_send()
        leave(k).wait()
    for copy in (state_out, hidden_out, cot_out, pre_out):
        copy.wait_send()
    for n, buf in enumerate((state, hidden, cots)):
        halo_sent(n, buf)
    for g in range(2):
        for part in range(3):
            for k in (1, 2, 3):
                for h in range(2):
                    step1(g, part, h, k).wait_send()
                    step2(g, part, h, k).wait_send()
            for k in range(1, 8):
                step3(g, part, k).wait_send()
        for k, cross in every5:
            step5(g, k, cross).wait_send()


def whole_step(state, truth, first, second):
    bf, f32 = jnp.bfloat16, jnp.float32
    dma = pltpu.SemaphoreType.DMA
    vmem = pltpu.VMEM
    block = vmem((6, 10, 16, 512), bf)
    scratch = [
        vmem((9, 512, 512), bf),
        vmem((9, 512, 512), bf),
        vmem((8, 2, 4, 8, 512), bf),
        vmem((4, 512, 128), f32),
        block,
        block,
        block,
        block,
        block,
        vmem((512, 512), f32),
        vmem((4, 512, 128), f32),
        vmem((8, 64, 512), bf),
        vmem((512, 512), bf),
        vmem((512, 512), bf),
        vmem((2, 512, 256), bf),
        vmem((4, 8, 512), bf),
        vmem((2, 256, 512), bf),
    ]
    for height in HEIGHT:
        scratch += [vmem((2, 4, 9, 4, height, 128), bf), vmem((2, 3, 9, 4, height, 128), bf)]
    for height in HEIGHT:
        scratch += [vmem((2, 4, 9, height, 128), bf), vmem((2, 3, 9, height, 128), bf)]
    scratch += [
        vmem((2, 2, 5, 16, 128), bf),
        vmem((2, 4, 5, 32, 128), bf),
        vmem((2, 8, 5, 32, 128), bf),
        vmem((2, 8, 5, 16, 128), bf),
    ]
    scratch += [dma((4,)), dma((4,)), dma((4,)), dma((3, 8)), dma((3, 8)), dma((2, 8)), dma((2, 8))]
    for dims in ((2, 6, 4), (2, 6, 4), (2, 3, 8), (2, 8)):
        scratch += [dma(dims), dma(dims)]
    in_vmem = pl.BlockSpec(memory_space=pltpu.VMEM)
    return pl.pallas_call(
        step_kernel,
        out_shape=[jax.ShapeDtypeStruct((8, 64, 512), bf), jax.ShapeDtypeStruct((2, 9, 16, 512), bf)],
        in_specs=[pl.BlockSpec(memory_space=pl.ANY)] * 4,
        out_specs=[in_vmem] * 2,
        scratch_shapes=scratch,
        compiler_params=pltpu.CompilerParams(collective_id=0, has_side_effects=True, vmem_limit_bytes=60 << 20),
        name="whole_step",
    )(state, truth, first, second)


def body(state, truth, conv_first, conv_second):
    members, rows, cols, channels = state.shape
    prognosis, slopes = whole_step(
        state, truth, jnp.transpose(conv_first, (1, 0, 2)), jnp.transpose(conv_second, (1, 0, 2))
    )
    prognosis = prognosis.reshape(8, members, rows, cols // 8, channels).transpose(1, 2, 0, 3, 4).reshape(state.shape)
    slopes = jnp.transpose(slopes.astype(jnp.float32), (0, 2, 1, 3))
    return prognosis, slopes[1], slopes[0]


def solution(mesh):
    in_specs = (P("member", "rows", None, None), P("rows", None, None), P(), P())
    out_specs = (P("member", "rows", None, None), P("rows", None, None), P("rows", None, None))
    return jax.shard_map(body, mesh=mesh, in_specs=in_specs, out_specs=out_specs, check_vma=False)
```

```python
import functools

import jax
import jax.numpy as jnp
from jax import lax
from jax.experimental import pallas as pl
from jax.experimental.pallas import tpu as pltpu
from jax.sharding import PartitionSpec as P

MESH = pl.DeviceIdType.MESH
EPS2 = 0.1 * 0.1
INV_ROOT_TWO = 0.7071067811865476
INV_ROOT_TWOPI = 0.3989422804014327


STARTS = (0, 4, 6, 8)
SIZES = (4, 2, 2, 1)
WIDE = 40
HEIGHT = (WIDE, 64 - WIDE)
AROUND = [(0, -1), (0, 1), (-1, -1), (-1, 1), (1, -1), (1, 1), (-1, 0), (1, 0)]


def step_kernel(state_hbm, truth_hbm, w1_hbm, w2_hbm, prog_ref, out_ref, *scratch):
    (w1, w2, stage, base, state, hidden, cots, state_sib, hidden_sib, slope, fore, leaving, cc, cp, csib, truth) = scratch[:16]
    (ct, sa, ra, sb, rb, ta, tra, tb, trb, um, uz, ur, fin) = scratch[16:29]
    (local, sibs, sibr, hsend, hrecv, asend, arecv, s1, r1, s2, r2, s3, r3, s5, r5) = scratch[29:]
    bf, f32 = jnp.bfloat16, jnp.float32
    member, rows = lax.axis_index("member"), lax.axis_index("rows")
    x, zh = member // 2, lax.rem(member, 2)
    y, z, c = rows // 8, lax.rem(rows // 2, 4), lax.rem(rows, 2)
    q = zh * 4 + x

    def at(px, pzh, py, pz, pc):
        return {"member": px * 2 + pzh, "rows": (py * 4 + pz) * 2 + pc}

    def holder(pq):
        return lax.rem(pq, 4) * 2 + pq // 4

    sibling = at(x, zh, y, z, 1 - c)

    def mate(k):
        return {"member": holder(lax.rem(q + k, 8)), "rows": rows}

    def near(dr, dq):
        return {"member": holder(lax.rem(q + dq + 8, 8)), "rows": lax.rem(rows + dr + 32, 32)}

    def along_y(k):
        return at(x, zh, lax.rem(y + k, 4), z, c)

    def along_x(k):
        return at(lax.rem(x + k, 4), zh, y, z, c)

    def cross_x(k):
        return at(lax.rem(x + k, 4), zh, y, z, 1 - c)

    ring = zh * 4 + z

    def along_z(k):
        to = lax.rem(ring + k, 8)
        return at(x, to // 4, y, lax.rem(to, 4), c)

    def send(src, dst, ssem, rsem, to):
        return pltpu.make_async_remote_copy(
            src_ref=src, dst_ref=dst, send_sem=ssem, recv_sem=rsem, device_id=to, device_id_type=MESH
        )

    load_w1 = pltpu.make_async_copy(w1_hbm, w1, local.at[0])
    load_w2 = pltpu.make_async_copy(w2_hbm, w2, local.at[1])
    load_w1.start()
    load_w2.start()

    barrier = pltpu.get_barrier_semaphore()
    peers = [mate(k) for k in range(1, 8)] + [along_z(k) for k in (1, 2, 3, 5, 6, 7)]
    peers += [near(dr, dq) for dr, dq in AROUND if dr]
    peers += [a(k) for a in (along_y, cross_x) for k in (1, 2, 3)]
    for p in peers:
        pl.semaphore_signal(barrier, inc=1, device_id=p, device_id_type=MESH)
    pl.semaphore_wait(barrier, len(peers))

    def columns(pq):
        return pl.ds(pl.multiple_of(pq * 8, 8), 8)

    own_state = pltpu.make_async_copy(state_hbm.at[:, :, columns(q)], stage.at[member], local.at[2])
    own_truth = pltpu.make_async_copy(truth_hbm.at[:, columns(q)], truth, local.at[3])

    def meet(k):
        to = lax.rem(q + k, 8)
        return send(state_hbm.at[:, :, columns(to)], stage.at[member], asend.at[0, k], arecv.at[0, k], mate(k))

    def leave(k):
        to = holder(lax.rem(q + k, 8))
        return send(leaving.at[to], prog_ref.at[q], asend.at[1, k], arecv.at[1, k], mate(k))

    far_first = (4, 3, 5, 2, 6, 1, 7)
    for k in far_first:
        meet(k).start()
    own_state.start()
    own_truth.start()

    def halo(n, buf, i):
        dr, dq = AROUND[i]

        def cut(step, size, low, high):
            return pl.ds(low, size) if step == 0 else pl.ds(high if step > 0 else low, 1)

        def edge(step, size):
            return pl.ds(1, size) if step == 0 else pl.ds(0 if step > 0 else size + 1, 1)

        return send(
            buf.at[cut(dr, 4, 1, 4), cut(dq, 8, 1, 8)],
            buf.at[edge(dr, 4), edge(dq, 8)],
            hsend.at[n, i],
            hrecv.at[n, i],
            near(dr, dq),
        )

    def inside(dr, dq):
        there = None
        for ok in [rows > 0] * (dr < 0) + [rows < 31] * (dr > 0) + [q > 0] * (dq < 0) + [q < 7] * (dq > 0):
            there = ok if there is None else jnp.logical_and(there, ok)
        return there

    def halo_start(n, buf):
        for i, (dr, dq) in enumerate(AROUND):
            @pl.when(inside(dr, dq))
            def _():
                halo(n, buf, i).start()

    def halo_sent(n, buf):
        for i, (dr, dq) in enumerate(AROUND):
            @pl.when(inside(dr, dq))
            def _():
                halo(n, buf, i).wait_send()

    def halo_wait(n, buf):
        for i, (dr, dq) in enumerate(AROUND):
            @pl.when(inside(-dr, -dq))
            def _():
                halo(n, buf, i).wait_recv()

        @pl.when(rows == 0)
        def _():
            buf[0] = jnp.zeros((10, 16, 512), bf)

        @pl.when(rows == 31)
        def _():
            buf[5] = jnp.zeros((10, 16, 512), bf)

        @pl.when(q == 0)
        def _():
            for r in range(6):
                buf[r, 0] = jnp.zeros((16, 512), bf)

        @pl.when(q == 7)
        def _():
            for r in range(6):
                buf[r, 9] = jnp.zeros((16, 512), bf)

    def view(buf, down, across):
        return buf[pl.ds(down, 4), pl.ds(across, 8)].reshape(512, 512)

    def turned(value):
        return jnp.transpose(value.astype(f32), (1, 0)).astype(bf)

    mine = pl.multiple_of(c * 256, 256)
    theirs = pl.multiple_of((1 - c) * 256, 256)
    state_out = send(state, state_sib, sibs.at[0], sibr.at[0], sibling)
    hidden_out = send(hidden, hidden_sib, sibs.at[1], sibr.at[1], sibling)
    cot_out = send(cc.at[:, pl.ds(theirs, 256)], csib.at[0], sibs.at[2], sibr.at[2], sibling)
    pre_out = send(cp.at[:, pl.ds(theirs, 256)], csib.at[1], sibs.at[3], sibr.at[3], sibling)

    def taps_of(part):
        return pl.ds(STARTS[part], SIZES[part])

    def pairs_of(part):
        return pl.ds(STARTS[part] // 2, (SIZES[part] + 1) // 2)

    def turn(h, s):
        here = y if h == 0 else x
        one, two = here + 1 - 2 * lax.rem(here, 2), 3 - here
        return (one, two) if s == 0 else (two, one)

    def on_axis(h, place):
        return at(x, zh, place, z, c) if h == 0 else at(place, zh, y, z, c)

    def step1(g, part, h, s, j):
        src, dst = (sa, ra) if h == 0 else (sb, rb)
        here = y if h == 0 else x
        one, two = turn(h, s)
        block = (one, lax.rem(here + 2, 4), two)[j]
        i = part * 4 + h * 2 + s
        return send(
            src.at[g, block, taps_of(part), pl.ds(s * 2, 2)],
            dst.at[g, j, taps_of(part), pl.ds(s * 2, 2)],
            s1.at[g, i, j],
            r1.at[g, i, j],
            on_axis(h, two if j == 2 else one),
        )

    def step2(g, part, h, k):
        s, r = (ta, tra) if h == 0 else (tb, trb)
        to = lax.rem((x if h == 0 else y) + k, 4)
        taps = taps_of(part)
        return send(
            s.at[g, to, taps],
            r.at[g, k - 1, taps],
            s2.at[g, part * 2 + h, k],
            r2.at[g, part * 2 + h, k],
            along_x(k) if h == 0 else along_y(k),
        )

    def step3(g, part, k):
        to = lax.rem(lax.rem(ring + k, 8), 4)
        pairs = pairs_of(part)
        return send(uz.at[g, to, pairs], ur.at[g, ring, pairs], s3.at[g, part, k], r3.at[g, part, k], along_z(k))

    spot = c * 4 + x

    def step5(g, piece, k, cross):
        pc = (1 - c) if cross else c
        to = (cross_x(k) if k else sibling) if cross else along_x(k)
        i = k + 4 * cross
        part = pl.ds(0, 4) if piece == 0 else pl.ds(4, 1)
        return send(um.at[g, pc, part], fin.at[g, spot, part], s5.at[g, piece, i], r5.at[g, piece, i], to)

    every5 = [(k, 0) for k in (2, 1, 3)] + [(k, 1) for k in (2, 1, 3, 0)]

    def form(g, part, own, sib):
        @pl.loop(STARTS[part], STARTS[part] + SIZES[part])
        def _(tap):
            down, across = tap // 3, lax.rem(tap, 3)
            total = jnp.dot(ct[0], view(own, down, across), preferred_element_type=f32)
            total = total + jnp.dot(ct[1], view(sib, down, across), preferred_element_type=f32)
            for xx in range(4):
                for yy in range(4):
                    for h in range(2):
                        top = xx * 64 + h * WIDE
                        piece = total[top : top + HEIGHT[h], yy * 128 : yy * 128 + 128].astype(bf)
                        if h == 0:
                            sa[g, yy, tap, xx] = piece
                        else:
                            sb[g, xx, tap, yy] = piece

        for j in (1, 0):
            for h in range(2):
                for half in range(2):
                    step1(g, part, h, half, j).start()

    def relay1(g, part):
        for h in range(2):
            own, got = ((sa, ra), (sb, rb))[h]
            for half in range(2):
                step1(g, part, h, half, 1).wait_recv()
                two = turn(h, half)[1]

                @pl.loop(STARTS[part], STARTS[part] + SIZES[part])
                def _(tap):
                    spot = (tap, slice(half * 2, half * 2 + 2))
                    total = own[(g, two) + spot].astype(f32) + got[(g, 1) + spot].astype(f32)
                    own[(g, two) + spot] = total.astype(bf)

                step1(g, part, h, half, 2).start()

    def summed(own, got, where):
        total = own[where].astype(f32)
        for k in range(3):
            total = total + got[(k,) + where].astype(f32)
        return total

    def add1(g, part):
        for h in range(2):
            for half in range(2):
                step1(g, part, h, half, 0).wait_recv()
                step1(g, part, h, half, 2).wait_recv()
            own, got, into = ((sa, ra, ta), (sb, rb, tb))[h]
            here = y if h == 0 else x

            @pl.loop(STARTS[part], STARTS[part] + SIZES[part])
            def _(tap):
                total = own[g, here, tap].astype(f32) + got[g, 0, tap].astype(f32) + got[g, 2, tap].astype(f32)
                total = total.astype(bf)
                for other in range(4):
                    into[g, other, tap] = total[other]

            for k in (2, 1, 3):
                step2(g, part, h, k).start()

    def add2(g, part):
        for h in range(2):
            for k in (1, 2, 3):
                step2(g, part, h, k).wait_recv()
        for pair in range(STARTS[part] // 2, STARTS[part] // 2 + (SIZES[part] + 1) // 2):
            blocks = []
            for tap in (2 * pair, 2 * pair + 1):
                for h in range(2):
                    own, got = ((ta, tra), (tb, trb))[h]
                    here = x if h == 0 else y
                    blocks.append(
                        summed(own.at[g, here], got.at[g], (tap,)) if tap < 9 else jnp.zeros((HEIGHT[h], 128), f32)
                    )
            flat = jnp.transpose(jnp.concatenate(blocks, axis=0), (1, 0)).astype(bf)
            for zz in range(4):
                uz[g, zz, pair] = flat[zz * 32 : zz * 32 + 32]
        for k in (4, 3, 5, 2, 6, 1, 7):
            step3(g, part, k).start()
        pairs = pairs_of(part)
        ur[g, ring, pairs] = uz[g, z, pairs]

    def add3(g, part):
        for k in range(1, 8):
            step3(g, part, k).wait_recv()
        pairs = slice(STARTS[part] // 2, STARTS[part] // 2 + (SIZES[part] + 1) // 2)
        total = ur[g, 0, pairs].astype(f32)
        for q in range(1, 8):
            total = total + ur[g, q, pairs].astype(f32)
        total = total.astype(bf)
        um[g, 0, pairs] = total[:, :16]
        um[g, 1, pairs] = total[:, 16:]

    def spread(g, piece):
        for k, cross in every5:
            step5(g, piece, k, cross).start()
        part = slice(0, 4) if piece == 0 else slice(4, 5)
        fin[g, spot, part] = um[g, c, part]

    def finish(g):
        for piece in range(2):
            for k, cross in every5:
                step5(g, piece, k, cross).wait_recv()
        for tap in range(9):
            off = (tap % 2) * 64
            row = [fin[g, i, tap // 2, :, off : off + 64] for i in range(8)]
            out_ref[g, tap] = jnp.concatenate(row, axis=1)

    own_state.wait()
    for k in range(1, 8):
        meet(k).wait_recv()

    @pl.loop(0, 8)
    def _(m):
        for j in range(2):
            for l in range(4):
                lanes = slice(l * 128, l * 128 + 128)
                value = stage[m, j, :, :, lanes].astype(f32).reshape(32, 128)
                base[l, pl.ds(m * 2 + j, 32, stride=16), :] = value

    for l in range(4):
        state[1:5, 1:9, :, l * 128 : l * 128 + 128] = base[l].astype(bf).reshape(4, 8, 16, 128)
    halo_start(0, state)
    load_w1.wait()
    halo_wait(0, state)
    state_out.start()

    def conv(buf, w, half):
        total = None
        for tap in range(9):
            term = jnp.dot(
                view(buf, tap // 3, tap % 3), w[tap, :, half * 256 : half * 256 + 256], preferred_element_type=f32
            )
            total = term if total is None else total + term
        return total

    for half in range(2):
        lanes = slice(half * 256, half * 256 + 256)
        pre = conv(state, w1, half)
        both = 0.5 * (1.0 + lax.erf(pre * INV_ROOT_TWO))
        slope[:, lanes] = both + pre * jnp.exp(-0.5 * pre * pre) * INV_ROOT_TWOPI
        hidden[1:5, 1:9, :, lanes] = (pre * both).astype(bf).reshape(4, 8, 16, 256)

    halo_start(1, hidden)
    load_w2.wait()
    halo_wait(1, hidden)
    hidden_out.start()
    for half in range(2):
        total = conv(hidden, w2, half)
        for l in range(2):
            fore[half * 2 + l] = base[half * 2 + l] + total[:, l * 128 : l * 128 + 128]

    for l in range(4):
        for k in range(16):
            value = fore[l, pl.ds(k, 32, stride=16), :]
            leaving[k // 2, (k % 2) * 32 : (k % 2) * 32 + 32, l * 128 : l * 128 + 128] = value.astype(bf)

    own_truth.wait()

    @pl.loop(0, 4)
    def _(l):
        @pl.loop(0, 4)
        def _(cell):
            fact = truth[cell, :, pl.ds(pl.multiple_of(l * 128, 128), 128)].astype(f32)

            def spot_of(k):
                return pl.ds(cell * 128 + k, 8, stride=16)

            xs = [fore[l, spot_of(k), :] for k in range(16)]
            pulls = [None] * 16

            def plus(i, v):
                pulls[i] = v if pulls[i] is None else pulls[i] + v

            for a in range(16):
                for b in range(a + 1, 16):
                    d = xs[a] - xs[b]
                    u = d * lax.rsqrt(d * d + EPS2)
                    plus(a, u)
                    plus(b, -u)
            for k in range(16):
                d = xs[k] - fact
                away = d * lax.rsqrt(d * d + EPS2)
                fore[l, spot_of(k), :] = away * (1.0 / 2048.0) - pulls[k] * (1.0 / 30720.0)

    for l in range(4):
        lanes = slice(l * 128, l * 128 + 128)
        value = fore[l].astype(bf)
        cc[:, lanes] = value
        cots[1:5, 1:9, :, lanes] = value.reshape(4, 8, 16, 128)
    cot_out.start()
    halo_start(2, cots)

    ct[0] = turned(cc[:, pl.ds(mine, 256)])
    cot_out.wait_recv()
    ct[1] = turned(csib[0])
    hidden_out.wait_recv()
    for part in range(4):
        form(0, part, hidden, hidden_sib)
    relay1(0, 0)

    halo_wait(2, cots)
    for k in far_first:
        leave(k).start()
    prog_ref[q] = leaving[member]
    for half in range(2):
        lanes = pl.ds(half * 256, 256)
        total = None
        for tap in range(9):
            term = lax.dot_general(
                view(cots, 2 - tap // 3, 2 - tap % 3),
                w2[tap, lanes],
                (((1,), (1,)), ((), ())),
                preferred_element_type=f32,
            )
            total = term if total is None else total + term
        cp[:, lanes] = (total * slope[:, lanes]).astype(bf)
        for part in ((1, 2), (3,))[half]:
            relay1(0, part)

    pre_out.start()
    ct[0] = turned(cp[:, pl.ds(mine, 256)])
    add1(0, 0)
    pre_out.wait_recv()
    ct[1] = turned(csib[1])
    state_out.wait_recv()
    form(1, 0, state, state_sib)
    add1(0, 1)
    form(1, 1, state, state_sib)
    add1(0, 2)
    add1(0, 3)
    form(1, 2, state, state_sib)
    form(1, 3, state, state_sib)
    relay1(1, 0)
    for part in range(4):
        add2(0, part)
    relay1(1, 1)
    relay1(1, 2)
    relay1(1, 3)
    add1(1, 0)
    for part in range(4):
        add3(0, part)
    spread(0, 0)
    spread(0, 1)
    add1(1, 1)
    add2(1, 0)
    add1(1, 2)
    add2(1, 1)
    add1(1, 3)
    add2(1, 2)
    add2(1, 3)
    for part in range(3):
        add3(1, part)
    spread(1, 0)
    finish(0)
    add3(1, 3)
    spread(1, 1)
    finish(1)

    for k in range(1, 8):
        meet(k).wait_send()
        leave(k).wait()
    for copy in (state_out, hidden_out, cot_out, pre_out):
        copy.wait_send()
    for n, buf in enumerate((state, hidden, cots)):
        halo_sent(n, buf)
    for g in range(2):
        for part in range(4):
            for h in range(2):
                for half in range(2):
                    for j in range(3):
                        step1(g, part, h, half, j).wait_send()
                for k in (1, 2, 3):
                    step2(g, part, h, k).wait_send()
            for k in range(1, 8):
                step3(g, part, k).wait_send()
        for piece in range(2):
            for k, cross in every5:
                step5(g, piece, k, cross).wait_send()


def whole_step(state, truth, first, second):
    bf, f32 = jnp.bfloat16, jnp.float32
    dma = pltpu.SemaphoreType.DMA
    vmem = pltpu.VMEM
    block = vmem((6, 10, 16, 512), bf)
    scratch = [
        vmem((9, 512, 512), bf),
        vmem((9, 512, 512), bf),
        vmem((8, 2, 4, 8, 512), bf),
        vmem((4, 512, 128), f32),
        block,
        block,
        block,
        block,
        block,
        vmem((512, 512), f32),
        vmem((4, 512, 128), f32),
        vmem((8, 64, 512), bf),
        vmem((512, 512), bf),
        vmem((512, 512), bf),
        vmem((2, 512, 256), bf),
        vmem((4, 8, 512), bf),
        vmem((2, 256, 512), bf),
    ]
    for height in HEIGHT:
        scratch += [vmem((2, 4, 9, 4, height, 128), bf), vmem((2, 3, 9, 4, height, 128), bf)]
    for height in HEIGHT:
        scratch += [vmem((2, 4, 9, height, 128), bf), vmem((2, 3, 9, height, 128), bf)]
    scratch += [
        vmem((2, 2, 5, 16, 128), bf),
        vmem((2, 4, 5, 32, 128), bf),
        vmem((2, 8, 5, 32, 128), bf),
        vmem((2, 8, 5, 16, 128), bf),
    ]
    scratch += [dma((4,)), dma((4,)), dma((4,)), dma((3, 8)), dma((3, 8)), dma((2, 8)), dma((2, 8))]
    for dims in ((2, 16, 3), (2, 8, 4), (2, 4, 8), (2, 2, 8)):
        scratch += [dma(dims), dma(dims)]
    in_vmem = pl.BlockSpec(memory_space=pltpu.VMEM)
    return pl.pallas_call(
        step_kernel,
        out_shape=[jax.ShapeDtypeStruct((8, 64, 512), bf), jax.ShapeDtypeStruct((2, 9, 16, 512), bf)],
        in_specs=[pl.BlockSpec(memory_space=pl.ANY)] * 4,
        out_specs=[in_vmem] * 2,
        scratch_shapes=scratch,
        compiler_params=pltpu.CompilerParams(collective_id=0, has_side_effects=True, vmem_limit_bytes=60 << 20),
        name="whole_step",
    )(state, truth, first, second)


def body(state, truth, conv_first, conv_second):
    members, rows, cols, channels = state.shape
    prognosis, slopes = whole_step(
        state, truth, jnp.transpose(conv_first, (1, 0, 2)), jnp.transpose(conv_second, (1, 0, 2))
    )
    prognosis = prognosis.reshape(8, members, rows, cols // 8, channels).transpose(1, 2, 0, 3, 4).reshape(state.shape)
    slopes = jnp.transpose(slopes.astype(jnp.float32), (0, 2, 1, 3))
    return prognosis, slopes[1], slopes[0]


def solution(mesh):
    in_specs = (P("member", "rows", None, None), P("rows", None, None), P(), P())
    out_specs = (P("member", "rows", None, None), P("rows", None, None), P("rows", None, None))
    return jax.shard_map(body, mesh=mesh, in_specs=in_specs, out_specs=out_specs, check_vma=False)
```

```python
import functools

import jax
import jax.numpy as jnp
from jax import lax
from jax.experimental import pallas as pl
from jax.experimental.pallas import tpu as pltpu
from jax.sharding import PartitionSpec as P

MESH = pl.DeviceIdType.MESH
EPS2 = 0.1 * 0.1
INV_ROOT_TWO = 0.7071067811865476
INV_ROOT_TWOPI = 0.3989422804014327


STARTS = (0, 4, 6, 8)
SIZES = (4, 2, 2, 1)
WIDE = 40
HEIGHT = (WIDE, 64 - WIDE)
AROUND = [(0, -1), (0, 1), (-1, -1), (-1, 1), (1, -1), (1, 1), (-1, 0), (1, 0)]


def step_kernel(state_hbm, truth_hbm, w1_hbm, w2_hbm, prog_ref, out_ref, *scratch):
    (w1, w2, stage, base, state, hidden, cots, state_sib, hidden_sib, slope, fore, leaving, cc, cp, csib, truth) = scratch[:16]
    (ct, sa, ra, sb, rb, ta, tra, tb, trb, um, uz, ur, fin) = scratch[16:29]
    (local, sibs, sibr, hsend, hrecv, asend, arecv, s1, r1, s2, r2, s3, r3, s5, r5) = scratch[29:]
    bf, f32 = jnp.bfloat16, jnp.float32
    member, rows = lax.axis_index("member"), lax.axis_index("rows")
    x, zh = member // 2, lax.rem(member, 2)
    y, z, c = rows // 8, lax.rem(rows // 2, 4), lax.rem(rows, 2)
    q = zh * 4 + x

    def at(px, pzh, py, pz, pc):
        return {"member": px * 2 + pzh, "rows": (py * 4 + pz) * 2 + pc}

    def holder(pq):
        return lax.rem(pq, 4) * 2 + pq // 4

    sibling = at(x, zh, y, z, 1 - c)

    def block_of(k):
        return lax.rem(x + k, 4) + 4 * (zh if k < 4 else 1 - zh)

    def mate(k):
        return {"member": holder(block_of(k)), "rows": rows}

    def near(dr, dq):
        return {"member": holder(lax.rem(q + dq + 8, 8)), "rows": lax.rem(rows + dr + 32, 32)}

    def along_y(k):
        return at(x, zh, lax.rem(y + k, 4), z, c)

    def along_x(k):
        return at(lax.rem(x + k, 4), zh, y, z, c)

    def cross_x(k):
        return at(lax.rem(x + k, 4), zh, y, z, 1 - c)

    ring = zh * 4 + z

    def along_z(k):
        to = lax.rem(ring + k, 8)
        return at(x, to // 4, y, lax.rem(to, 4), c)

    def send(src, dst, ssem, rsem, to):
        return pltpu.make_async_remote_copy(
            src_ref=src, dst_ref=dst, send_sem=ssem, recv_sem=rsem, device_id=to, device_id_type=MESH
        )

    load_w1 = pltpu.make_async_copy(w1_hbm, w1, local.at[0])
    load_w2 = pltpu.make_async_copy(w2_hbm, w2, local.at[1])
    load_w1.start()
    load_w2.start()

    barrier = pltpu.get_barrier_semaphore()
    peers = [mate(k) for k in range(1, 8)] + [along_z(k) for k in (1, 2, 3, 5, 6, 7)]
    peers += [near(dr, dq) for dr, dq in AROUND if dr]
    peers += [a(k) for a in (along_y, cross_x) for k in (1, 2, 3)]
    for p in peers:
        pl.semaphore_signal(barrier, inc=1, device_id=p, device_id_type=MESH)
    pl.semaphore_wait(barrier, len(peers))

    def columns(pq):
        return pl.ds(pl.multiple_of(pq * 8, 8), 8)

    own_state = pltpu.make_async_copy(state_hbm.at[:, :, columns(q)], stage.at[member], local.at[2])
    own_truth = pltpu.make_async_copy(truth_hbm.at[:, columns(q)], truth, local.at[3])

    def meet(k):
        to = block_of(k)
        return send(state_hbm.at[:, :, columns(to)], stage.at[member], asend.at[0, k], arecv.at[0, k], mate(k))

    def leave(k):
        to = holder(block_of(k))
        return send(leaving.at[to], prog_ref.at[q], asend.at[1, k], arecv.at[1, k], mate(k))

    far_first = (6, 5, 7, 4, 2, 1, 3)
    for k in far_first:
        meet(k).start()
    own_state.start()
    own_truth.start()

    def halo(n, buf, part, i):
        lanes = pl.ds(part * 256, 256)
        dr, dq = AROUND[i]

        def cut(step, size, low, high):
            return pl.ds(low, size) if step == 0 else pl.ds(high if step > 0 else low, 1)

        def edge(step, size):
            return pl.ds(1, size) if step == 0 else pl.ds(0 if step > 0 else size + 1, 1)

        return send(
            buf.at[cut(dr, 4, 1, 4), cut(dq, 8, 1, 8), :, lanes],
            buf.at[edge(dr, 4), edge(dq, 8), :, lanes],
            hsend.at[n, part, i],
            hrecv.at[n, part, i],
            near(dr, dq),
        )

    def inside(dr, dq):
        there = None
        for ok in [rows > 0] * (dr < 0) + [rows < 31] * (dr > 0) + [q > 0] * (dq < 0) + [q < 7] * (dq > 0):
            there = ok if there is None else jnp.logical_and(there, ok)
        return there

    def halo_start(n, buf, part):
        for i, (dr, dq) in enumerate(AROUND):
            @pl.when(inside(dr, dq))
            def _():
                halo(n, buf, part, i).start()

    def halo_sent(n, buf, part):
        for i, (dr, dq) in enumerate(AROUND):
            @pl.when(inside(dr, dq))
            def _():
                halo(n, buf, part, i).wait_send()

    def halo_wait(n, buf, part):
        for i, (dr, dq) in enumerate(AROUND):
            @pl.when(inside(-dr, -dq))
            def _():
                halo(n, buf, part, i).wait_recv()

    def view(buf, down, across):
        return buf[pl.ds(down, 4), pl.ds(across, 8)].reshape(512, 512)

    def turned(value):
        return jnp.transpose(value.astype(f32), (1, 0)).astype(bf)

    mine = pl.multiple_of(c * 256, 256)
    theirs = pl.multiple_of((1 - c) * 256, 256)
    state_out = send(state, state_sib, sibs.at[0], sibr.at[0], sibling)
    hidden_out = send(hidden, hidden_sib, sibs.at[1], sibr.at[1], sibling)
    cot_out = send(cc.at[:, pl.ds(theirs, 256)], csib.at[0], sibs.at[2], sibr.at[2], sibling)
    pre_out = send(cp.at[:, pl.ds(theirs, 256)], csib.at[1], sibs.at[3], sibr.at[3], sibling)

    def taps_of(part):
        return pl.ds(STARTS[part], SIZES[part])

    def pairs_of(part):
        return pl.ds(STARTS[part] // 2, (SIZES[part] + 1) // 2)

    def turn(h, s):
        here = y if h == 0 else x
        one, two = here + 1 - 2 * lax.rem(here, 2), 3 - here
        return (one, two) if s == 0 else (two, one)

    def on_axis(h, place):
        return at(x, zh, place, z, c) if h == 0 else at(place, zh, y, z, c)

    def step1(g, part, h, s, j):
        src, dst = (sa, ra) if h == 0 else (sb, rb)
        here = y if h == 0 else x
        one, two = turn(h, s)
        block = (one, lax.rem(here + 2, 4), two)[j]
        i = part * 4 + h * 2 + s
        return send(
            src.at[g, block, taps_of(part), pl.ds(s * 2, 2)],
            dst.at[g, j, taps_of(part), pl.ds(s * 2, 2)],
            s1.at[g, i, j],
            r1.at[g, i, j],
            on_axis(h, two if j == 2 else one),
        )

    def step2(g, part, h, k):
        s, r = (ta, tra) if h == 0 else (tb, trb)
        to = lax.rem((x if h == 0 else y) + k, 4)
        taps = taps_of(part)
        return send(
            s.at[g, to, taps],
            r.at[g, k - 1, taps],
            s2.at[g, part * 2 + h, k],
            r2.at[g, part * 2 + h, k],
            along_x(k) if h == 0 else along_y(k),
        )

    def step3(g, part, k):
        to = lax.rem(lax.rem(ring + k, 8), 4)
        pairs = pairs_of(part)
        return send(uz.at[g, to, pairs], ur.at[g, ring, pairs], s3.at[g, part, k], r3.at[g, part, k], along_z(k))

    spot = c * 4 + x

    def step5(g, piece, k, cross):
        pc = (1 - c) if cross else c
        to = (cross_x(k) if k else sibling) if cross else along_x(k)
        i = k + 4 * cross
        part = pl.ds(0, 4) if piece == 0 else pl.ds(4, 1)
        return send(um.at[g, pc, part], fin.at[g, spot, part], s5.at[g, piece, i], r5.at[g, piece, i], to)

    every5 = [(k, 0) for k in (2, 1, 3)] + [(k, 1) for k in (2, 1, 3, 0)]

    def form(g, part, own, sib):
        @pl.loop(STARTS[part], STARTS[part] + SIZES[part])
        def _(tap):
            down, across = tap // 3, lax.rem(tap, 3)
            total = jnp.dot(ct[0], view(own, down, across), preferred_element_type=f32)
            total = total + jnp.dot(ct[1], view(sib, down, across), preferred_element_type=f32)
            for xx in range(4):
                for yy in range(4):
                    for h in range(2):
                        top = xx * 64 + h * WIDE
                        piece = total[top : top + HEIGHT[h], yy * 128 : yy * 128 + 128].astype(bf)
                        if h == 0:
                            sa[g, yy, tap, xx] = piece
                        else:
                            sb[g, xx, tap, yy] = piece

        for j in (1, 0):
            for h in range(2):
                for half in range(2):
                    step1(g, part, h, half, j).start()

    def relay1(g, part):
        for h in range(2):
            own, got = ((sa, ra), (sb, rb))[h]
            for half in range(2):
                step1(g, part, h, half, 1).wait_recv()
                two = turn(h, half)[1]

                @pl.loop(STARTS[part], STARTS[part] + SIZES[part])
                def _(tap):
                    spot = (tap, slice(half * 2, half * 2 + 2))
                    total = own[(g, two) + spot].astype(f32) + got[(g, 1) + spot].astype(f32)
                    own[(g, two) + spot] = total.astype(bf)

                step1(g, part, h, half, 2).start()

    def summed(own, got, where):
        total = own[where].astype(f32)
        for k in range(3):
            total = total + got[(k,) + where].astype(f32)
        return total

    def add1(g, part):
        for h in range(2):
            for half in range(2):
                step1(g, part, h, half, 0).wait_recv()
                step1(g, part, h, half, 2).wait_recv()
            own, got, into = ((sa, ra, ta), (sb, rb, tb))[h]
            here = y if h == 0 else x

            @pl.loop(STARTS[part], STARTS[part] + SIZES[part])
            def _(tap):
                total = own[g, here, tap].astype(f32) + got[g, 0, tap].astype(f32) + got[g, 2, tap].astype(f32)
                total = total.astype(bf)
                for other in range(4):
                    into[g, other, tap] = total[other]

            for k in (2, 1, 3):
                step2(g, part, h, k).start()

    def add2(g, part):
        for h in range(2):
            for k in (1, 2, 3):
                step2(g, part, h, k).wait_recv()
        for pair in range(STARTS[part] // 2, STARTS[part] // 2 + (SIZES[part] + 1) // 2):
            blocks = []
            for tap in (2 * pair, 2 * pair + 1):
                for h in range(2):
                    own, got = ((ta, tra), (tb, trb))[h]
                    here = x if h == 0 else y
                    blocks.append(
                        summed(own.at[g, here], got.at[g], (tap,)) if tap < 9 else jnp.zeros((HEIGHT[h], 128), f32)
                    )
            flat = jnp.transpose(jnp.concatenate(blocks, axis=0), (1, 0)).astype(bf)
            for zz in range(4):
                uz[g, zz, pair] = flat[zz * 32 : zz * 32 + 32]
        for k in (4, 3, 5, 2, 6, 1, 7):
            step3(g, part, k).start()
        pairs = pairs_of(part)
        ur[g, ring, pairs] = uz[g, z, pairs]

    def add3(g, part):
        for k in range(1, 8):
            step3(g, part, k).wait_recv()
        pairs = slice(STARTS[part] // 2, STARTS[part] // 2 + (SIZES[part] + 1) // 2)
        total = ur[g, 0, pairs].astype(f32)
        for q in range(1, 8):
            total = total + ur[g, q, pairs].astype(f32)
        total = total.astype(bf)
        um[g, 0, pairs] = total[:, :16]
        um[g, 1, pairs] = total[:, 16:]

    def spread(g, piece):
        for k, cross in every5:
            step5(g, piece, k, cross).start()
        part = slice(0, 4) if piece == 0 else slice(4, 5)
        fin[g, spot, part] = um[g, c, part]

    def finish(g):
        for piece in range(2):
            for k, cross in every5:
                step5(g, piece, k, cross).wait_recv()
        for tap in range(9):
            off = (tap % 2) * 64
            row = [fin[g, i, tap // 2, :, off : off + 64] for i in range(8)]
            out_ref[g, tap] = jnp.concatenate(row, axis=1)

    for buf in (state, hidden, cots):

        @pl.when(rows == 0)
        def _():
            buf[0] = jnp.zeros((10, 16, 512), bf)

        @pl.when(rows == 31)
        def _():
            buf[5] = jnp.zeros((10, 16, 512), bf)

        @pl.when(q == 0)
        def _():
            for r in range(6):
                buf[r, 0] = jnp.zeros((16, 512), bf)

        @pl.when(q == 7)
        def _():
            for r in range(6):
                buf[r, 9] = jnp.zeros((16, 512), bf)

    own_state.wait()
    for k in range(1, 8):
        meet(k).wait_recv()

    @pl.loop(0, 8)
    def _(m):
        for j in range(2):
            for l in range(4):
                lanes = slice(l * 128, l * 128 + 128)
                value = stage[m, j, :, :, lanes].astype(f32).reshape(32, 128)
                base[l, pl.ds(m * 2 + j, 32, stride=16), :] = value

    for l in range(4):
        state[1:5, 1:9, :, l * 128 : l * 128 + 128] = base[l].astype(bf).reshape(4, 8, 16, 128)
    halo_start(0, state, 0)
    halo_start(0, state, 1)
    load_w1.wait()

    def conv(buf, w, half, part):
        total = None
        for tap in range(9):
            piece = buf[pl.ds(tap // 3, 4), pl.ds(tap % 3, 8), :, part * 256 : part * 256 + 256].reshape(512, 256)
            term = jnp.dot(
                piece,
                w[tap, part * 256 : part * 256 + 256, half * 256 : half * 256 + 256],
                preferred_element_type=f32,
            )
            total = term if total is None else total + term
        return total

    halo_wait(0, state, 0)
    for half in range(2):
        slope[:, half * 256 : half * 256 + 256] = conv(state, w1, half, 0)
    halo_wait(0, state, 1)
    state_out.start()
    for half in range(2):
        lanes = slice(half * 256, half * 256 + 256)
        pre = slope[:, lanes] + conv(state, w1, half, 1)
        both = 0.5 * (1.0 + lax.erf(pre * INV_ROOT_TWO))
        slope[:, lanes] = both + pre * jnp.exp(-0.5 * pre * pre) * INV_ROOT_TWOPI
        hidden[1:5, 1:9, :, lanes] = (pre * both).astype(bf).reshape(4, 8, 16, 256)
        halo_start(1, hidden, half)

    load_w2.wait()
    for part in range(2):
        halo_wait(1, hidden, part)
        if part == 1:
            hidden_out.start()
        for half in range(2):
            total = conv(hidden, w2, half, part)
            for l in range(2):
                before = (base, fore)[part][half * 2 + l]
                fore[half * 2 + l] = before + total[:, l * 128 : l * 128 + 128]

    for l in range(4):
        for k in range(16):
            value = fore[l, pl.ds(k, 32, stride=16), :]
            leaving[k // 2, (k % 2) * 32 : (k % 2) * 32 + 32, l * 128 : l * 128 + 128] = value.astype(bf)

    for k in (2, 1, 3):
        leave(k).start()

    own_truth.wait()

    @pl.loop(0, 4)
    def _(l):
        @pl.loop(0, 4)
        def _(cell):
            fact = truth[cell, :, pl.ds(pl.multiple_of(l * 128, 128), 128)].astype(f32)

            def spot_of(k):
                return pl.ds(cell * 128 + k, 8, stride=16)

            xs = [fore[l, spot_of(k), :] for k in range(16)]
            pulls = [None] * 16

            def plus(i, v):
                pulls[i] = v if pulls[i] is None else pulls[i] + v

            for a in range(16):
                for b in range(a + 1, 16):
                    d = xs[a] - xs[b]
                    u = d * lax.rsqrt(d * d + EPS2)
                    plus(a, u)
                    plus(b, -u)
            for k in range(16):
                d = xs[k] - fact
                away = d * lax.rsqrt(d * d + EPS2)
                fore[l, spot_of(k), :] = away * (1.0 / 2048.0) - pulls[k] * (1.0 / 30720.0)

    for l in range(4):
        lanes = slice(l * 128, l * 128 + 128)
        value = fore[l].astype(bf)
        cc[:, lanes] = value
        cots[1:5, 1:9, :, lanes] = value.reshape(4, 8, 16, 128)
    cot_out.start()
    halo_start(2, cots, 0)
    halo_start(2, cots, 1)

    ct[0] = turned(cc[:, pl.ds(mine, 256)])
    cot_out.wait_recv()
    ct[1] = turned(csib[0])
    hidden_out.wait_recv()
    for part in range(4):
        form(0, part, hidden, hidden_sib)
    relay1(0, 0)

    halo_wait(2, cots, 0)
    halo_wait(2, cots, 1)
    for k in (6, 5, 7, 4):
        leave(k).start()
    prog_ref[q] = leaving[member]
    for half in range(2):
        lanes = pl.ds(half * 256, 256)
        total = None
        for tap in range(9):
            term = lax.dot_general(
                view(cots, 2 - tap // 3, 2 - tap % 3),
                w2[tap, lanes],
                (((1,), (1,)), ((), ())),
                preferred_element_type=f32,
            )
            total = term if total is None else total + term
        cp[:, lanes] = (total * slope[:, lanes]).astype(bf)
        for part in ((1, 2), (3,))[half]:
            relay1(0, part)

    pre_out.start()
    ct[0] = turned(cp[:, pl.ds(mine, 256)])
    add1(0, 0)
    pre_out.wait_recv()
    ct[1] = turned(csib[1])
    state_out.wait_recv()
    form(1, 0, state, state_sib)
    add1(0, 1)
    form(1, 1, state, state_sib)
    add1(0, 2)
    add1(0, 3)
    form(1, 2, state, state_sib)
    form(1, 3, state, state_sib)
    relay1(1, 0)
    for part in range(4):
        add2(0, part)
    relay1(1, 1)
    relay1(1, 2)
    relay1(1, 3)
    add1(1, 0)
    for part in range(4):
        add3(0, part)
    spread(0, 0)
    spread(0, 1)
    add1(1, 1)
    add2(1, 0)
    add1(1, 2)
    add2(1, 1)
    add1(1, 3)
    add2(1, 2)
    add2(1, 3)
    for part in range(3):
        add3(1, part)
    spread(1, 0)
    finish(0)
    add3(1, 3)
    spread(1, 1)
    finish(1)

    for k in range(1, 8):
        meet(k).wait_send()
        leave(k).wait()
    for copy in (state_out, hidden_out, cot_out, pre_out):
        copy.wait_send()
    for n, buf in enumerate((state, hidden, cots)):
        halo_sent(n, buf, 0)
        halo_sent(n, buf, 1)
    for g in range(2):
        for part in range(4):
            for h in range(2):
                for half in range(2):
                    for j in range(3):
                        step1(g, part, h, half, j).wait_send()
                for k in (1, 2, 3):
                    step2(g, part, h, k).wait_send()
            for k in range(1, 8):
                step3(g, part, k).wait_send()
        for piece in range(2):
            for k, cross in every5:
                step5(g, piece, k, cross).wait_send()


def whole_step(state, truth, first, second):
    bf, f32 = jnp.bfloat16, jnp.float32
    dma = pltpu.SemaphoreType.DMA
    vmem = pltpu.VMEM
    block = vmem((6, 10, 16, 512), bf)
    scratch = [
        vmem((9, 512, 512), bf),
        vmem((9, 512, 512), bf),
        vmem((8, 2, 4, 8, 512), bf),
        vmem((4, 512, 128), f32),
        block,
        block,
        block,
        block,
        block,
        vmem((512, 512), f32),
        vmem((4, 512, 128), f32),
        vmem((8, 64, 512), bf),
        vmem((512, 512), bf),
        vmem((512, 512), bf),
        vmem((2, 512, 256), bf),
        vmem((4, 8, 512), bf),
        vmem((2, 256, 512), bf),
    ]
    for height in HEIGHT:
        scratch += [vmem((2, 4, 9, 4, height, 128), bf), vmem((2, 3, 9, 4, height, 128), bf)]
    for height in HEIGHT:
        scratch += [vmem((2, 4, 9, height, 128), bf), vmem((2, 3, 9, height, 128), bf)]
    scratch += [
        vmem((2, 2, 5, 16, 128), bf),
        vmem((2, 4, 5, 32, 128), bf),
        vmem((2, 8, 5, 32, 128), bf),
        vmem((2, 8, 5, 16, 128), bf),
    ]
    scratch += [dma((4,)), dma((4,)), dma((4,)), dma((3, 2, 8)), dma((3, 2, 8)), dma((2, 8)), dma((2, 8))]
    for dims in ((2, 16, 3), (2, 8, 4), (2, 4, 8), (2, 2, 8)):
        scratch += [dma(dims), dma(dims)]
    in_vmem = pl.BlockSpec(memory_space=pltpu.VMEM)
    return pl.pallas_call(
        step_kernel,
        out_shape=[jax.ShapeDtypeStruct((8, 64, 512), bf), jax.ShapeDtypeStruct((2, 9, 16, 512), bf)],
        in_specs=[pl.BlockSpec(memory_space=pl.ANY)] * 4,
        out_specs=[in_vmem] * 2,
        scratch_shapes=scratch,
        compiler_params=pltpu.CompilerParams(collective_id=0, has_side_effects=True, vmem_limit_bytes=60 << 20),
        name="whole_step",
    )(state, truth, first, second)


def body(state, truth, conv_first, conv_second):
    members, rows, cols, channels = state.shape
    prognosis, slopes = whole_step(
        state, truth, jnp.transpose(conv_first, (1, 0, 2)), jnp.transpose(conv_second, (1, 0, 2))
    )
    prognosis = prognosis.reshape(8, members, rows, cols // 8, channels).transpose(1, 2, 0, 3, 4).reshape(state.shape)
    second, first = [jnp.transpose(slopes[g], (1, 0, 2)).astype(jnp.float32) for g in range(2)]
    return prognosis, first, second


def solution(mesh):
    in_specs = (P("member", "rows", None, None), P("rows", None, None), P(), P())
    out_specs = (P("member", "rows", None, None), P("rows", None, None), P("rows", None, None))
    return jax.shard_map(body, mesh=mesh, in_specs=in_specs, out_specs=out_specs, check_vma=False)
```

```python
import functools

import jax
import jax.numpy as jnp
from jax import lax
from jax.experimental import pallas as pl
from jax.experimental.pallas import tpu as pltpu
from jax.sharding import PartitionSpec as P

MESH = pl.DeviceIdType.MESH
EPS2 = 0.1 * 0.1
INV_ROOT_TWO = 0.7071067811865476
INV_ROOT_TWOPI = 0.3989422804014327


STARTS = (0, 4, 6, 8)
SIZES = (4, 2, 2, 1)
WIDE = 40
HEIGHT = (WIDE, 64 - WIDE)
AROUND = [(0, -1), (0, 1), (-1, -1), (-1, 1), (1, -1), (1, 1), (-1, 0), (1, 0)]


def step_kernel(state_hbm, truth_hbm, w1_hbm, w2_hbm, prog_ref, out_ref, *scratch):
    (w1, w2, stage, base, state, hidden, cots, state_sib, hidden_sib, slope, fore, leaving, cc, cp, csib, truth) = scratch[:16]
    (ct, sa, ra, sb, rb, ta, tra, tb, trb, um, uz, ur, fin) = scratch[16:29]
    (local, sibs, sibr, hsend, hrecv, asend, arecv, s1, r1, s2, r2, s3, r3, s5, r5) = scratch[29:]
    bf, f32 = jnp.bfloat16, jnp.float32
    member, rows = lax.axis_index("member"), lax.axis_index("rows")
    x, zh = member // 2, lax.rem(member, 2)
    y, z, c = rows // 8, lax.rem(rows // 2, 4), lax.rem(rows, 2)
    q = zh * 4 + x

    def at(px, pzh, py, pz, pc):
        return {"member": px * 2 + pzh, "rows": (py * 4 + pz) * 2 + pc}

    def holder(pq):
        return lax.rem(pq, 4) * 2 + pq // 4

    sibling = at(x, zh, y, z, 1 - c)

    def block_of(k):
        return lax.rem(x + k, 4) + 4 * (zh if k < 4 else 1 - zh)

    def mate(k):
        return {"member": holder(block_of(k)), "rows": rows}

    def near(dr, dq):
        return {"member": holder(lax.rem(q + dq + 8, 8)), "rows": lax.rem(rows + dr + 32, 32)}

    def along_y(k):
        return at(x, zh, lax.rem(y + k, 4), z, c)

    def along_x(k):
        return at(lax.rem(x + k, 4), zh, y, z, c)

    def cross_x(k):
        return at(lax.rem(x + k, 4), zh, y, z, 1 - c)

    ring = zh * 4 + z

    def along_z(k):
        to = lax.rem(ring + k, 8)
        return at(x, to // 4, y, lax.rem(to, 4), c)

    def send(src, dst, ssem, rsem, to):
        return pltpu.make_async_remote_copy(
            src_ref=src, dst_ref=dst, send_sem=ssem, recv_sem=rsem, device_id=to, device_id_type=MESH
        )

    load_w1 = pltpu.make_async_copy(w1_hbm, w1, local.at[0])
    load_w2 = pltpu.make_async_copy(w2_hbm, w2, local.at[1])
    load_w1.start()
    load_w2.start()

    barrier = pltpu.get_barrier_semaphore()
    peers = [mate(k) for k in range(1, 8)] + [along_z(k) for k in (1, 2, 3, 5, 6, 7)]
    peers += [near(dr, dq) for dr, dq in AROUND if dr]
    peers += [a(k) for a in (along_y, cross_x) for k in (1, 2, 3)]
    for p in peers:
        pl.semaphore_signal(barrier, inc=1, device_id=p, device_id_type=MESH)
    pl.semaphore_wait(barrier, len(peers))

    def columns(pq):
        return pl.ds(pl.multiple_of(pq * 8, 8), 8)

    own_state = pltpu.make_async_copy(state_hbm.at[:, :, columns(q)], stage.at[member], local.at[2])
    own_truth = pltpu.make_async_copy(truth_hbm.at[:, columns(q)], truth, local.at[3])

    def meet(k):
        to = block_of(k)
        return send(state_hbm.at[:, :, columns(to)], stage.at[member], asend.at[0, k], arecv.at[0, k], mate(k))

    def leave(k):
        to = holder(block_of(k))
        return send(leaving.at[to], prog_ref.at[q], asend.at[1, k], arecv.at[1, k], mate(k))

    far_first = (6, 5, 7, 4, 2, 1, 3)
    for k in far_first:
        meet(k).start()
    own_state.start()
    own_truth.start()

    def halo(n, buf, part, i):
        lanes = pl.ds(pl.multiple_of(part * 256, 256) if not isinstance(part, int) else part * 256, 256)
        dr, dq = AROUND[i]

        def cut(step, size, low, high):
            return pl.ds(low, size) if step == 0 else pl.ds(high if step > 0 else low, 1)

        def edge(step, size):
            return pl.ds(1, size) if step == 0 else pl.ds(0 if step > 0 else size + 1, 1)

        return send(
            buf.at[cut(dr, 4, 1, 4), cut(dq, 8, 1, 8), :, lanes],
            buf.at[edge(dr, 4), edge(dq, 8), :, lanes],
            hsend.at[n, part, i],
            hrecv.at[n, part, i],
            near(dr, dq),
        )

    def inside(dr, dq):
        there = None
        for ok in [rows > 0] * (dr < 0) + [rows < 31] * (dr > 0) + [q > 0] * (dq < 0) + [q < 7] * (dq > 0):
            there = ok if there is None else jnp.logical_and(there, ok)
        return there

    def halo_start(n, buf, part):
        for i, (dr, dq) in enumerate(AROUND):
            @pl.when(inside(dr, dq))
            def _():
                halo(n, buf, part, i).start()

    def halo_sent(n, buf, part):
        for i, (dr, dq) in enumerate(AROUND):
            @pl.when(inside(dr, dq))
            def _():
                halo(n, buf, part, i).wait_send()

    def halo_wait(n, buf, part):
        for i, (dr, dq) in enumerate(AROUND):
            @pl.when(inside(-dr, -dq))
            def _():
                halo(n, buf, part, i).wait_recv()

    def view(buf, down, across):
        return buf[pl.ds(down, 4), pl.ds(across, 8)].reshape(512, 512)

    def turned(value):
        return jnp.transpose(value.astype(f32), (1, 0)).astype(bf)

    mine = pl.multiple_of(c * 256, 256)
    theirs = pl.multiple_of((1 - c) * 256, 256)
    state_out = send(state, state_sib, sibs.at[0], sibr.at[0], sibling)
    hidden_out = send(hidden, hidden_sib, sibs.at[1], sibr.at[1], sibling)
    cot_out = send(cc.at[:, pl.ds(theirs, 256)], csib.at[0], sibs.at[2], sibr.at[2], sibling)
    pre_out = send(cp.at[:, pl.ds(theirs, 256)], csib.at[1], sibs.at[3], sibr.at[3], sibling)

    def taps_of(part):
        return pl.ds(STARTS[part], SIZES[part])

    def pairs_of(part):
        return pl.ds(STARTS[part] // 2, (SIZES[part] + 1) // 2)

    def turn(h, s):
        here = y if h == 0 else x
        one, two = here + 1 - 2 * lax.rem(here, 2), 3 - here
        return (one, two) if s == 0 else (two, one)

    def on_axis(h, place):
        return at(x, zh, place, z, c) if h == 0 else at(place, zh, y, z, c)

    def step1(g, part, h, s, j):
        src, dst = (sa, ra) if h == 0 else (sb, rb)
        here = y if h == 0 else x
        one, two = turn(h, s)
        block = (one, lax.rem(here + 2, 4), two)[j]
        i = part * 4 + h * 2 + s
        return send(
            src.at[g, block, taps_of(part), pl.ds(s * 2, 2)],
            dst.at[g, j, taps_of(part), pl.ds(s * 2, 2)],
            s1.at[g, i, j],
            r1.at[g, i, j],
            on_axis(h, two if j == 2 else one),
        )

    def step2(g, part, h, k):
        s, r = (ta, tra) if h == 0 else (tb, trb)
        to = lax.rem((x if h == 0 else y) + k, 4)
        taps = taps_of(part)
        return send(
            s.at[g, to, taps],
            r.at[g, k - 1, taps],
            s2.at[g, part * 2 + h, k],
            r2.at[g, part * 2 + h, k],
            along_x(k) if h == 0 else along_y(k),
        )

    def step3(g, part, k):
        to = lax.rem(lax.rem(ring + k, 8), 4)
        pairs = pairs_of(part)
        return send(uz.at[g, to, pairs], ur.at[g, ring, pairs], s3.at[g, part, k], r3.at[g, part, k], along_z(k))

    spot = c * 4 + x

    def step5(g, piece, k, cross):
        pc = (1 - c) if cross else c
        to = (cross_x(k) if k else sibling) if cross else along_x(k)
        i = k + 4 * cross
        part = pl.ds(0, 4) if piece == 0 else pl.ds(4, 1)
        return send(um.at[g, pc, part], fin.at[g, spot, part], s5.at[g, piece, i], r5.at[g, piece, i], to)

    every5 = [(k, 0) for k in (2, 1, 3)] + [(k, 1) for k in (2, 1, 3, 0)]

    def form(g, part, own, sib):
        @pl.loop(STARTS[part], STARTS[part] + SIZES[part])
        def _(tap):
            down, across = tap // 3, lax.rem(tap, 3)
            total = jnp.dot(ct[0], view(own, down, across), preferred_element_type=f32)
            total = total + jnp.dot(ct[1], view(sib, down, across), preferred_element_type=f32)
            for xx in range(4):
                for yy in range(4):
                    for h in range(2):
                        top = xx * 64 + h * WIDE
                        piece = total[top : top + HEIGHT[h], yy * 128 : yy * 128 + 128].astype(bf)
                        if h == 0:
                            sa[g, yy, tap, xx] = piece
                        else:
                            sb[g, xx, tap, yy] = piece

        for j in (1, 0):
            for h in range(2):
                for half in range(2):
                    step1(g, part, h, half, j).start()

    def relay1(g, part):
        for h in range(2):
            own, got = ((sa, ra), (sb, rb))[h]
            for half in range(2):
                step1(g, part, h, half, 1).wait_recv()
                two = turn(h, half)[1]

                @pl.loop(STARTS[part], STARTS[part] + SIZES[part])
                def _(tap):
                    spot = (tap, slice(half * 2, half * 2 + 2))
                    total = own[(g, two) + spot].astype(f32) + got[(g, 1) + spot].astype(f32)
                    own[(g, two) + spot] = total.astype(bf)

                step1(g, part, h, half, 2).start()

    def summed(own, got, where):
        total = own[where].astype(f32)
        for k in range(3):
            total = total + got[(k,) + where].astype(f32)
        return total

    def add1(g, part):
        for h in range(2):
            for half in range(2):
                step1(g, part, h, half, 0).wait_recv()
                step1(g, part, h, half, 2).wait_recv()
            own, got, into = ((sa, ra, ta), (sb, rb, tb))[h]
            here = y if h == 0 else x

            @pl.loop(STARTS[part], STARTS[part] + SIZES[part])
            def _(tap):
                total = own[g, here, tap].astype(f32) + got[g, 0, tap].astype(f32) + got[g, 2, tap].astype(f32)
                total = total.astype(bf)
                for other in range(4):
                    into[g, other, tap] = total[other]

            for k in (2, 1, 3):
                step2(g, part, h, k).start()

    def add2(g, part):
        for h in range(2):
            for k in (1, 2, 3):
                step2(g, part, h, k).wait_recv()
        for pair in range(STARTS[part] // 2, STARTS[part] // 2 + (SIZES[part] + 1) // 2):
            blocks = []
            for tap in (2 * pair, 2 * pair + 1):
                for h in range(2):
                    own, got = ((ta, tra), (tb, trb))[h]
                    here = x if h == 0 else y
                    blocks.append(
                        summed(own.at[g, here], got.at[g], (tap,)) if tap < 9 else jnp.zeros((HEIGHT[h], 128), f32)
                    )
            flat = jnp.transpose(jnp.concatenate(blocks, axis=0), (1, 0)).astype(bf)
            for zz in range(4):
                uz[g, zz, pair] = flat[zz * 32 : zz * 32 + 32]
        for k in (4, 3, 5, 2, 6, 1, 7):
            step3(g, part, k).start()
        pairs = pairs_of(part)
        ur[g, ring, pairs] = uz[g, z, pairs]

    def add3(g, part):
        for k in range(1, 8):
            step3(g, part, k).wait_recv()
        pairs = slice(STARTS[part] // 2, STARTS[part] // 2 + (SIZES[part] + 1) // 2)
        total = ur[g, 0, pairs].astype(f32)
        for q in range(1, 8):
            total = total + ur[g, q, pairs].astype(f32)
        total = total.astype(bf)
        um[g, 0, pairs] = total[:, :16]
        um[g, 1, pairs] = total[:, 16:]

    def spread(g, piece):
        for k, cross in every5:
            step5(g, piece, k, cross).start()
        part = slice(0, 4) if piece == 0 else slice(4, 5)
        fin[g, spot, part] = um[g, c, part]

    def finish(g):
        for piece in range(2):
            for k, cross in every5:
                step5(g, piece, k, cross).wait_recv()
        for tap in range(9):
            off = (tap % 2) * 64
            row = [fin[g, i, tap // 2, :, off : off + 64] for i in range(8)]
            out_ref[g, tap] = jnp.concatenate(row, axis=1)

    for buf in (state, hidden, cots):

        @pl.when(rows == 0)
        def _():
            buf[0] = jnp.zeros((10, 16, 512), bf)

        @pl.when(rows == 31)
        def _():
            buf[5] = jnp.zeros((10, 16, 512), bf)

        @pl.when(q == 0)
        def _():
            for r in range(6):
                buf[r, 0] = jnp.zeros((16, 512), bf)

        @pl.when(q == 7)
        def _():
            for r in range(6):
                buf[r, 9] = jnp.zeros((16, 512), bf)

    own_state.wait()
    for k in range(1, 8):
        meet(k).wait_recv()

    @pl.loop(0, 8)
    def _(m):
        for j in range(2):
            for l in range(4):
                lanes = slice(l * 128, l * 128 + 128)
                value = stage[m, j, :, :, lanes].astype(f32).reshape(32, 128)
                base[l, pl.ds(m * 2 + j, 32, stride=16), :] = value

    for l in range(4):
        state[1:5, 1:9, :, l * 128 : l * 128 + 128] = base[l].astype(bf).reshape(4, 8, 16, 128)
    halo_start(0, state, 0)
    halo_start(0, state, 1)
    load_w1.wait()

    def conv(buf, w, half, part):
        total = None
        for tap in range(9):
            piece = buf[pl.ds(tap // 3, 4), pl.ds(tap % 3, 8), :, part * 256 : part * 256 + 256].reshape(512, 256)
            term = jnp.dot(
                piece,
                w[tap, part * 256 : part * 256 + 256, half * 256 : half * 256 + 256],
                preferred_element_type=f32,
            )
            total = term if total is None else total + term
        return total

    halo_wait(0, state, 0)
    for half in range(2):
        slope[:, half * 256 : half * 256 + 256] = conv(state, w1, half, 0)
    halo_wait(0, state, 1)
    state_out.start()
    for half in range(2):
        lanes = slice(half * 256, half * 256 + 256)
        pre = slope[:, lanes] + conv(state, w1, half, 1)
        both = 0.5 * (1.0 + lax.erf(pre * INV_ROOT_TWO))
        slope[:, lanes] = both + pre * jnp.exp(-0.5 * pre * pre) * INV_ROOT_TWOPI
        hidden[1:5, 1:9, :, lanes] = (pre * both).astype(bf).reshape(4, 8, 16, 256)
        halo_start(1, hidden, half)

    load_w2.wait()
    for part in range(2):
        halo_wait(1, hidden, part)
        if part == 1:
            hidden_out.start()
        for half in range(2):
            total = conv(hidden, w2, half, part)
            for l in range(2):
                before = (base, fore)[part][half * 2 + l]
                fore[half * 2 + l] = before + total[:, l * 128 : l * 128 + 128]

    for l in range(4):
        for k in range(16):
            value = fore[l, pl.ds(k, 32, stride=16), :]
            leaving[k // 2, (k % 2) * 32 : (k % 2) * 32 + 32, l * 128 : l * 128 + 128] = value.astype(bf)

    for k in (2, 1, 3):
        leave(k).start()

    own_truth.wait()

    for part, to_sibling in ((1 - c, True), (c, False)):

        @pl.loop(part * 2, part * 2 + 2)
        def _(l):
            @pl.loop(0, 4)
            def _(cell):
                fact = truth[cell, :, pl.ds(pl.multiple_of(l * 128, 128), 128)].astype(f32)

                def spot_of(k):
                    return pl.ds(cell * 128 + k, 8, stride=16)

                xs = [fore[l, spot_of(k), :] for k in range(16)]
                pulls = [None] * 16

                def plus(i, v):
                    pulls[i] = v if pulls[i] is None else pulls[i] + v

                for a in range(16):
                    for b in range(a + 1, 16):
                        d = xs[a] - xs[b]
                        u = d * lax.rsqrt(d * d + EPS2)
                        plus(a, u)
                        plus(b, -u)
                for k in range(16):
                    d = xs[k] - fact
                    away = d * lax.rsqrt(d * d + EPS2)
                    fore[l, spot_of(k), :] = away * (1.0 / 2048.0) - pulls[k] * (1.0 / 30720.0)

        for i in range(2):
            lanes = pl.ds(pl.multiple_of(part * 256 + i * 128, 128), 128)
            value = fore[part * 2 + i].astype(bf)
            cc[:, lanes] = value
            cots[1:5, 1:9, :, lanes] = value.reshape(4, 8, 16, 128)
        if to_sibling:
            cot_out.start()
        halo_start(2, cots, part)

    ct[0] = turned(cc[:, pl.ds(mine, 256)])
    cot_out.wait_recv()
    ct[1] = turned(csib[0])
    hidden_out.wait_recv()
    for part in range(4):
        form(0, part, hidden, hidden_sib)
    relay1(0, 0)

    def adjoint(i_lanes, part):
        total = None
        for tap in range(9):
            down, across = 2 - tap // 3, 2 - tap % 3
            o_lanes = slice(part * 256, part * 256 + 256)
            piece = cots[down : down + 4, across : across + 8, :, o_lanes].reshape(512, 256)
            term = lax.dot_general(
                piece, w2[tap, i_lanes, o_lanes], (((1,), (1,)), ((), ())), preferred_element_type=f32
            )
            total = term if total is None else total + term
        return total

    halo_wait(2, cots, 0)
    for i, start in enumerate((theirs, mine)):
        total = adjoint(pl.ds(start, 256), 0)
        for l in range(2):
            base[i * 2 + l] = total[:, l * 128 : l * 128 + 128]
    halo_wait(2, cots, 1)
    for i, start in enumerate((theirs, mine)):
        total = jnp.concatenate([base[i * 2], base[i * 2 + 1]], axis=1) + adjoint(pl.ds(start, 256), 1)
        cp[:, pl.ds(start, 256)] = (total * slope[:, pl.ds(start, 256)]).astype(bf)
        if i == 0:
            pre_out.start()
            relay1(0, 1)
    for k in (6, 5, 7, 4):
        leave(k).start()
    prog_ref[q] = leaving[member]
    relay1(0, 2)
    relay1(0, 3)

    ct[0] = turned(cp[:, pl.ds(mine, 256)])
    add1(0, 0)
    pre_out.wait_recv()
    ct[1] = turned(csib[1])
    state_out.wait_recv()
    form(1, 0, state, state_sib)
    add1(0, 1)
    form(1, 1, state, state_sib)
    add1(0, 2)
    add1(0, 3)
    form(1, 2, state, state_sib)
    form(1, 3, state, state_sib)
    relay1(1, 0)
    for part in range(4):
        add2(0, part)
    relay1(1, 1)
    relay1(1, 2)
    relay1(1, 3)
    add1(1, 0)
    for part in range(4):
        add3(0, part)
    spread(0, 0)
    spread(0, 1)
    add1(1, 1)
    add2(1, 0)
    add1(1, 2)
    add2(1, 1)
    add1(1, 3)
    add2(1, 2)
    add2(1, 3)
    for part in range(3):
        add3(1, part)
    spread(1, 0)
    finish(0)
    add3(1, 3)
    spread(1, 1)
    finish(1)

    for k in range(1, 8):
        meet(k).wait_send()
        leave(k).wait()
    for copy in (state_out, hidden_out, cot_out, pre_out):
        copy.wait_send()
    for n, buf in enumerate((state, hidden, cots)):
        halo_sent(n, buf, 0)
        halo_sent(n, buf, 1)
    for g in range(2):
        for part in range(4):
            for h in range(2):
                for half in range(2):
                    for j in range(3):
                        step1(g, part, h, half, j).wait_send()
                for k in (1, 2, 3):
                    step2(g, part, h, k).wait_send()
            for k in range(1, 8):
                step3(g, part, k).wait_send()
        for piece in range(2):
            for k, cross in every5:
                step5(g, piece, k, cross).wait_send()


def whole_step(state, truth, first, second):
    bf, f32 = jnp.bfloat16, jnp.float32
    dma = pltpu.SemaphoreType.DMA
    vmem = pltpu.VMEM
    block = vmem((6, 10, 16, 512), bf)
    scratch = [
        vmem((9, 512, 512), bf),
        vmem((9, 512, 512), bf),
        vmem((8, 2, 4, 8, 512), bf),
        vmem((4, 512, 128), f32),
        block,
        block,
        block,
        block,
        block,
        vmem((512, 512), f32),
        vmem((4, 512, 128), f32),
        vmem((8, 64, 512), bf),
        vmem((512, 512), bf),
        vmem((512, 512), bf),
        vmem((2, 512, 256), bf),
        vmem((4, 8, 512), bf),
        vmem((2, 256, 512), bf),
    ]
    for height in HEIGHT:
        scratch += [vmem((2, 4, 9, 4, height, 128), bf), vmem((2, 3, 9, 4, height, 128), bf)]
    for height in HEIGHT:
        scratch += [vmem((2, 4, 9, height, 128), bf), vmem((2, 3, 9, height, 128), bf)]
    scratch += [
        vmem((2, 2, 5, 16, 128), bf),
        vmem((2, 4, 5, 32, 128), bf),
        vmem((2, 8, 5, 32, 128), bf),
        vmem((2, 8, 5, 16, 128), bf),
    ]
    scratch += [dma((4,)), dma((4,)), dma((4,)), dma((3, 2, 8)), dma((3, 2, 8)), dma((2, 8)), dma((2, 8))]
    for dims in ((2, 16, 3), (2, 8, 4), (2, 4, 8), (2, 2, 8)):
        scratch += [dma(dims), dma(dims)]
    in_vmem = pl.BlockSpec(memory_space=pltpu.VMEM)
    return pl.pallas_call(
        step_kernel,
        out_shape=[jax.ShapeDtypeStruct((8, 64, 512), bf), jax.ShapeDtypeStruct((2, 9, 16, 512), bf)],
        in_specs=[pl.BlockSpec(memory_space=pl.ANY)] * 4,
        out_specs=[in_vmem] * 2,
        scratch_shapes=scratch,
        compiler_params=pltpu.CompilerParams(collective_id=0, has_side_effects=True, vmem_limit_bytes=60 << 20),
        name="whole_step",
    )(state, truth, first, second)


def body(state, truth, conv_first, conv_second):
    members, rows, cols, channels = state.shape
    prognosis, slopes = whole_step(
        state, truth, jnp.transpose(conv_first, (1, 0, 2)), jnp.transpose(conv_second, (1, 0, 2))
    )
    prognosis = prognosis.reshape(8, members, rows, cols // 8, channels).transpose(1, 2, 0, 3, 4).reshape(state.shape)
    second, first = [jnp.transpose(slopes[g], (1, 0, 2)).astype(jnp.float32) for g in range(2)]
    return prognosis, first, second


def solution(mesh):
    in_specs = (P("member", "rows", None, None), P("rows", None, None), P(), P())
    out_specs = (P("member", "rows", None, None), P("rows", None, None), P("rows", None, None))
    return jax.shard_map(body, mesh=mesh, in_specs=in_specs, out_specs=out_specs, check_vma=False)
```

```python
import functools

import jax
import jax.numpy as jnp
from jax import lax
from jax.experimental import pallas as pl
from jax.experimental.pallas import tpu as pltpu
from jax.sharding import PartitionSpec as P

MESH = pl.DeviceIdType.MESH
EPS2 = 0.1 * 0.1
INV_ROOT_TWO = 0.7071067811865476
INV_ROOT_TWOPI = 0.3989422804014327


STARTS = (0, 4, 6, 8)
SIZES = (4, 2, 2, 1)
WIDE = 40
HEIGHT = (WIDE, 64 - WIDE)
AROUND = [(0, -1), (0, 1), (-1, -1), (-1, 1), (1, -1), (1, 1), (-1, 0), (1, 0)]


def step_kernel(state_hbm, truth_hbm, w1_hbm, w2_hbm, prog_ref, out_ref, *scratch):
    (w1, w2, stage, base, state, hidden, cots, state_sib, hidden_sib, slope, fore, leaving, cc, cp, csib, truth) = scratch[:16]
    (ct, sa, ra, sb, rb, ta, tra, tb, trb, um, uz, ur, fin) = scratch[16:29]
    (local, sibs, sibr, hsend, hrecv, asend, arecv, s1, r1, s2, r2, s3, r3, s5, r5) = scratch[29:]
    bf, f32 = jnp.bfloat16, jnp.float32
    member, rows = lax.axis_index("member"), lax.axis_index("rows")
    x, zh = member // 2, lax.rem(member, 2)
    y, z, c = rows // 8, lax.rem(rows // 2, 4), lax.rem(rows, 2)
    q = zh * 4 + x

    def at(px, pzh, py, pz, pc):
        return {"member": px * 2 + pzh, "rows": (py * 4 + pz) * 2 + pc}

    def holder(pq):
        return lax.rem(pq, 4) * 2 + pq // 4

    sibling = at(x, zh, y, z, 1 - c)

    def block_of(k):
        return lax.rem(x + k, 4) + 4 * (zh if k < 4 else 1 - zh)

    def mate(k):
        return {"member": holder(block_of(k)), "rows": rows}

    def near(dr, dq):
        return {"member": holder(lax.rem(q + dq + 8, 8)), "rows": lax.rem(rows + dr + 32, 32)}

    def along_y(k):
        return at(x, zh, lax.rem(y + k, 4), z, c)

    def along_x(k):
        return at(lax.rem(x + k, 4), zh, y, z, c)

    def cross_x(k):
        return at(lax.rem(x + k, 4), zh, y, z, 1 - c)

    ring = zh * 4 + z

    def along_z(k):
        to = lax.rem(ring + k, 8)
        return at(x, to // 4, y, lax.rem(to, 4), c)

    def send(src, dst, ssem, rsem, to):
        return pltpu.make_async_remote_copy(
            src_ref=src, dst_ref=dst, send_sem=ssem, recv_sem=rsem, device_id=to, device_id_type=MESH
        )

    load_w1 = pltpu.make_async_copy(w1_hbm, w1, local.at[0])
    load_w2 = pltpu.make_async_copy(w2_hbm, w2, local.at[1])
    load_w1.start()
    load_w2.start()

    barrier = pltpu.get_barrier_semaphore()
    peers = [mate(k) for k in range(1, 8)] + [along_z(k) for k in (1, 2, 3, 5, 6, 7)]
    peers += [near(dr, dq) for dr, dq in AROUND if dr]
    peers += [a(k) for a in (along_y, cross_x) for k in (1, 2, 3)]
    for p in peers:
        pl.semaphore_signal(barrier, inc=1, device_id=p, device_id_type=MESH)
    pl.semaphore_wait(barrier, len(peers))

    def columns(pq):
        return pl.ds(pl.multiple_of(pq * 8, 8), 8)

    own_state = pltpu.make_async_copy(state_hbm.at[:, :, columns(q)], stage.at[member], local.at[2])
    own_truth = pltpu.make_async_copy(truth_hbm.at[:, columns(q)], truth, local.at[3])

    def meet(k):
        to = block_of(k)
        return send(state_hbm.at[:, :, columns(to)], stage.at[member], asend.at[0, k], arecv.at[0, k], mate(k))

    def leave(k):
        to = holder(block_of(k))
        return send(leaving.at[to], prog_ref.at[q], asend.at[1, k], arecv.at[1, k], mate(k))

    far_first = (6, 5, 7, 4, 2, 1, 3)
    for k in far_first:
        meet(k).start()
    own_state.start()
    own_truth.start()

    def halo(n, buf, part, i):
        lanes = pl.ds(pl.multiple_of(part * 256, 256) if not isinstance(part, int) else part * 256, 256)
        dr, dq = AROUND[i]

        def cut(step, size, low, high):
            return pl.ds(low, size) if step == 0 else pl.ds(high if step > 0 else low, 1)

        def edge(step, size):
            return pl.ds(1, size) if step == 0 else pl.ds(0 if step > 0 else size + 1, 1)

        return send(
            buf.at[cut(dr, 4, 1, 4), cut(dq, 8, 1, 8), :, lanes],
            buf.at[edge(dr, 4), edge(dq, 8), :, lanes],
            hsend.at[n, part, i],
            hrecv.at[n, part, i],
            near(dr, dq),
        )

    def inside(dr, dq):
        there = None
        for ok in [rows > 0] * (dr < 0) + [rows < 31] * (dr > 0) + [q > 0] * (dq < 0) + [q < 7] * (dq > 0):
            there = ok if there is None else jnp.logical_and(there, ok)
        return there

    def halo_start(n, buf, part):
        for i, (dr, dq) in enumerate(AROUND):
            @pl.when(inside(dr, dq))
            def _():
                halo(n, buf, part, i).start()

    def halo_sent(n, buf, part):
        for i, (dr, dq) in enumerate(AROUND):
            @pl.when(inside(dr, dq))
            def _():
                halo(n, buf, part, i).wait_send()

    def halo_wait(n, buf, part):
        for i, (dr, dq) in enumerate(AROUND):
            @pl.when(inside(-dr, -dq))
            def _():
                halo(n, buf, part, i).wait_recv()

    def view(buf, down, across):
        return buf[pl.ds(down, 4), pl.ds(across, 8)].reshape(512, 512)

    def turned(value):
        return jnp.transpose(value.astype(f32), (1, 0)).astype(bf)

    mine = pl.multiple_of(c * 256, 256)
    theirs = pl.multiple_of((1 - c) * 256, 256)
    state_out = send(state, state_sib, sibs.at[0], sibr.at[0], sibling)
    hidden_out = send(hidden, hidden_sib, sibs.at[1], sibr.at[1], sibling)
    cot_out = send(cc.at[:, pl.ds(theirs, 256)], csib.at[0], sibs.at[2], sibr.at[2], sibling)
    pre_out = send(cp.at[:, pl.ds(theirs, 256)], csib.at[1], sibs.at[3], sibr.at[3], sibling)

    def taps_of(part):
        return pl.ds(STARTS[part], SIZES[part])

    def pairs_of(part):
        return pl.ds(STARTS[part] // 2, (SIZES[part] + 1) // 2)

    def turn(h, s):
        here = y if h == 0 else x
        one, two = here + 1 - 2 * lax.rem(here, 2), 3 - here
        return (one, two) if s == 0 else (two, one)

    def on_axis(h, place):
        return at(x, zh, place, z, c) if h == 0 else at(place, zh, y, z, c)

    def step1(g, part, h, s, j):
        src, dst = (sa, ra) if h == 0 else (sb, rb)
        here = y if h == 0 else x
        one, two = turn(h, s)
        block = (one, lax.rem(here + 2, 4), two)[j]
        i = part * 4 + h * 2 + s
        return send(
            src.at[g, block, taps_of(part), pl.ds(s * 2, 2)],
            dst.at[g, j, taps_of(part), pl.ds(s * 2, 2)],
            s1.at[g, i, j],
            r1.at[g, i, j],
            on_axis(h, two if j == 2 else one),
        )

    def step2(g, part, h, k):
        s, r = (ta, tra) if h == 0 else (tb, trb)
        to = lax.rem((x if h == 0 else y) + k, 4)
        taps = taps_of(part)
        return send(
            s.at[g, to, taps],
            r.at[g, k - 1, taps],
            s2.at[g, part * 2 + h, k],
            r2.at[g, part * 2 + h, k],
            along_x(k) if h == 0 else along_y(k),
        )

    def step3(g, part, k):
        to = lax.rem(lax.rem(ring + k, 8), 4)
        pairs = pairs_of(part)
        return send(uz.at[g, to, pairs], ur.at[g, ring, pairs], s3.at[g, part, k], r3.at[g, part, k], along_z(k))

    spot = c * 4 + x

    def step5(g, piece, k, cross):
        pc = (1 - c) if cross else c
        to = (cross_x(k) if k else sibling) if cross else along_x(k)
        i = k + 4 * cross
        part = pl.ds(0, 4) if piece == 0 else pl.ds(4, 1)
        return send(um.at[g, pc, part], fin.at[g, spot, part], s5.at[g, piece, i], r5.at[g, piece, i], to)

    every5 = [(k, 0) for k in (2, 1, 3)] + [(k, 1) for k in (2, 1, 3, 0)]

    def form(g, part, own, sib):
        @pl.loop(STARTS[part], STARTS[part] + SIZES[part])
        def _(tap):
            down, across = tap // 3, lax.rem(tap, 3)
            total = jnp.dot(ct[0], view(own, down, across), preferred_element_type=f32)
            total = total + jnp.dot(ct[1], view(sib, down, across), preferred_element_type=f32)
            for xx in range(4):
                for yy in range(4):
                    for h in range(2):
                        top = xx * 64 + h * WIDE
                        piece = total[top : top + HEIGHT[h], yy * 128 : yy * 128 + 128].astype(bf)
                        if h == 0:
                            sa[g, yy, tap, xx] = piece
                        else:
                            sb[g, xx, tap, yy] = piece

        for j in (1, 0):
            for h in range(2):
                for half in range(2):
                    step1(g, part, h, half, j).start()

    def relay1(g, part):
        for h in range(2):
            own, got = ((sa, ra), (sb, rb))[h]
            for half in range(2):
                step1(g, part, h, half, 1).wait_recv()
                two = turn(h, half)[1]

                @pl.loop(STARTS[part], STARTS[part] + SIZES[part])
                def _(tap):
                    spot = (tap, slice(half * 2, half * 2 + 2))
                    total = own[(g, two) + spot].astype(f32) + got[(g, 1) + spot].astype(f32)
                    own[(g, two) + spot] = total.astype(bf)

                step1(g, part, h, half, 2).start()

    def summed(own, got, where):
        total = own[where].astype(f32)
        for k in range(3):
            total = total + got[(k,) + where].astype(f32)
        return total

    def add1(g, part):
        for h in range(2):
            for half in range(2):
                step1(g, part, h, half, 0).wait_recv()
                step1(g, part, h, half, 2).wait_recv()
            own, got, into = ((sa, ra, ta), (sb, rb, tb))[h]
            here = y if h == 0 else x

            @pl.loop(STARTS[part], STARTS[part] + SIZES[part])
            def _(tap):
                total = own[g, here, tap].astype(f32) + got[g, 0, tap].astype(f32) + got[g, 2, tap].astype(f32)
                total = total.astype(bf)
                for other in range(4):
                    into[g, other, tap] = total[other]

            for k in (2, 1, 3):
                step2(g, part, h, k).start()

    def add2(g, part):
        for h in range(2):
            for k in (1, 2, 3):
                step2(g, part, h, k).wait_recv()
        for pair in range(STARTS[part] // 2, STARTS[part] // 2 + (SIZES[part] + 1) // 2):
            blocks = []
            for tap in (2 * pair, 2 * pair + 1):
                for h in range(2):
                    own, got = ((ta, tra), (tb, trb))[h]
                    here = x if h == 0 else y
                    blocks.append(
                        summed(own.at[g, here], got.at[g], (tap,)) if tap < 9 else jnp.zeros((HEIGHT[h], 128), f32)
                    )
            flat = jnp.transpose(jnp.concatenate(blocks, axis=0), (1, 0)).astype(bf)
            for zz in range(4):
                uz[g, zz, pair] = flat[zz * 32 : zz * 32 + 32]
        for k in (4, 3, 5, 2, 6, 1, 7):
            step3(g, part, k).start()
        pairs = pairs_of(part)
        ur[g, ring, pairs] = uz[g, z, pairs]

    def add3(g, part):
        for k in range(1, 8):
            step3(g, part, k).wait_recv()
        pairs = slice(STARTS[part] // 2, STARTS[part] // 2 + (SIZES[part] + 1) // 2)
        total = ur[g, 0, pairs].astype(f32)
        for q in range(1, 8):
            total = total + ur[g, q, pairs].astype(f32)
        total = total.astype(bf)
        um[g, 0, pairs] = total[:, :16]
        um[g, 1, pairs] = total[:, 16:]

    def spread(g, piece):
        for k, cross in every5:
            step5(g, piece, k, cross).start()
        part = slice(0, 4) if piece == 0 else slice(4, 5)
        fin[g, spot, part] = um[g, c, part]

    def finish(g):
        for piece in range(2):
            for k, cross in every5:
                step5(g, piece, k, cross).wait_recv()
        for tap in range(9):
            off = (tap % 2) * 64
            row = [fin[g, i, tap // 2, :, off : off + 64] for i in range(8)]
            out_ref[g, tap] = jnp.concatenate(row, axis=1)

    for buf in (state, hidden, cots):

        @pl.when(rows == 0)
        def _():
            buf[0] = jnp.zeros((10, 16, 512), bf)

        @pl.when(rows == 31)
        def _():
            buf[5] = jnp.zeros((10, 16, 512), bf)

        @pl.when(q == 0)
        def _():
            for r in range(6):
                buf[r, 0] = jnp.zeros((16, 512), bf)

        @pl.when(q == 7)
        def _():
            for r in range(6):
                buf[r, 9] = jnp.zeros((16, 512), bf)

    own_state.wait()
    for k in range(1, 8):
        meet(k).wait_recv()

    @pl.loop(0, 8)
    def _(m):
        for j in range(2):
            for l in range(4):
                lanes = slice(l * 128, l * 128 + 128)
                value = stage[m, j, :, :, lanes].astype(f32).reshape(32, 128)
                base[l, pl.ds(m * 2 + j, 32, stride=16), :] = value

    for l in range(4):
        state[1:5, 1:9, :, l * 128 : l * 128 + 128] = base[l].astype(bf).reshape(4, 8, 16, 128)
    halo_start(0, state, 0)
    halo_start(0, state, 1)
    load_w1.wait()

    def conv(buf, w, half, part):
        total = None
        for tap in range(9):
            piece = buf[pl.ds(tap // 3, 4), pl.ds(tap % 3, 8), :, part * 256 : part * 256 + 256].reshape(512, 256)
            term = jnp.dot(
                piece,
                w[tap, part * 256 : part * 256 + 256, half * 256 : half * 256 + 256],
                preferred_element_type=f32,
            )
            total = term if total is None else total + term
        return total

    halo_wait(0, state, 0)
    for half in range(2):
        slope[:, half * 256 : half * 256 + 256] = conv(state, w1, half, 0)
    halo_wait(0, state, 1)
    state_out.start()
    for half in range(2):
        lanes = slice(half * 256, half * 256 + 256)
        pre = slope[:, lanes] + conv(state, w1, half, 1)
        both = 0.5 * (1.0 + lax.erf(pre * INV_ROOT_TWO))
        slope[:, lanes] = both + pre * jnp.exp(-0.5 * pre * pre) * INV_ROOT_TWOPI
        hidden[1:5, 1:9, :, lanes] = (pre * both).astype(bf).reshape(4, 8, 16, 256)
        halo_start(1, hidden, half)

    load_w2.wait()
    for part in range(2):
        halo_wait(1, hidden, part)
        if part == 1:
            hidden_out.start()
        for half in range(2):
            total = conv(hidden, w2, half, part)
            for l in range(2):
                before = (base, fore)[part][half * 2 + l]
                fore[half * 2 + l] = before + total[:, l * 128 : l * 128 + 128]

    for l in range(4):
        for k in range(16):
            value = fore[l, pl.ds(k, 32, stride=16), :]
            leaving[k // 2, (k % 2) * 32 : (k % 2) * 32 + 32, l * 128 : l * 128 + 128] = value.astype(bf)

    for k in (2, 1, 3):
        leave(k).start()

    own_truth.wait()

    for part, to_sibling in ((1 - c, True), (c, False)):

        @pl.loop(part * 2, part * 2 + 2)
        def _(l):
            @pl.loop(0, 4)
            def _(cell):
                fact = truth[cell, :, pl.ds(pl.multiple_of(l * 128, 128), 128)].astype(f32)

                def spot_of(k):
                    return pl.ds(cell * 128 + k, 8, stride=16)

                xs = [fore[l, spot_of(k), :] for k in range(16)]
                pulls = [None] * 16

                def plus(i, v):
                    pulls[i] = v if pulls[i] is None else pulls[i] + v

                for a in range(16):
                    for b in range(a + 1, 16):
                        d = xs[a] - xs[b]
                        u = d * lax.rsqrt(d * d + EPS2)
                        plus(a, u)
                        plus(b, -u)
                for k in range(16):
                    d = xs[k] - fact
                    away = d * lax.rsqrt(d * d + EPS2)
                    fore[l, spot_of(k), :] = away * (1.0 / 2048.0) - pulls[k] * (1.0 / 30720.0)

        for i in range(2):
            lanes = pl.ds(pl.multiple_of(part * 256 + i * 128, 128), 128)
            value = fore[part * 2 + i].astype(bf)
            cc[:, lanes] = value
            cots[1:5, 1:9, :, lanes] = value.reshape(4, 8, 16, 128)
        if to_sibling:
            cot_out.start()
        halo_start(2, cots, part)

    ct[0] = turned(cc[:, pl.ds(mine, 256)])
    cot_out.wait_recv()
    ct[1] = turned(csib[0])
    hidden_out.wait_recv()
    for part in range(4):
        form(0, part, hidden, hidden_sib)
    relay1(0, 0)

    def adjoint(i_lanes, part):
        total = None
        for tap in range(9):
            down, across = 2 - tap // 3, 2 - tap % 3
            o_lanes = slice(part * 256, part * 256 + 256)
            piece = cots[down : down + 4, across : across + 8, :, o_lanes].reshape(512, 256)
            term = lax.dot_general(
                piece, w2[tap, i_lanes, o_lanes], (((1,), (1,)), ((), ())), preferred_element_type=f32
            )
            total = term if total is None else total + term
        return total

    halo_wait(2, cots, 0)
    for i, start in enumerate((theirs, mine)):
        total = adjoint(pl.ds(start, 256), 0)
        for l in range(2):
            base[i * 2 + l] = total[:, l * 128 : l * 128 + 128]
    halo_wait(2, cots, 1)
    for i, start in enumerate((theirs, mine)):
        total = jnp.concatenate([base[i * 2], base[i * 2 + 1]], axis=1) + adjoint(pl.ds(start, 256), 1)
        cp[:, pl.ds(start, 256)] = (total * slope[:, pl.ds(start, 256)]).astype(bf)
        if i == 0:
            pre_out.start()
            relay1(0, 1)
    for k in (6, 5, 7, 4):
        leave(k).start()
    prog_ref[q] = leaving[member]
    relay1(0, 2)
    relay1(0, 3)

    ct[0] = turned(cp[:, pl.ds(mine, 256)])
    add1(0, 0)
    pre_out.wait_recv()
    ct[1] = turned(csib[1])
    state_out.wait_recv()
    form(1, 0, state, state_sib)
    add1(0, 1)
    form(1, 1, state, state_sib)
    add1(0, 2)
    add1(0, 3)
    form(1, 2, state, state_sib)
    form(1, 3, state, state_sib)
    relay1(1, 0)
    for part in range(4):
        add2(0, part)
    relay1(1, 1)
    relay1(1, 2)
    relay1(1, 3)
    add1(1, 0)
    add1(1, 1)
    add2(1, 0)
    for part in range(4):
        add3(0, part)
    spread(0, 0)
    spread(0, 1)
    add1(1, 2)
    add2(1, 1)
    add1(1, 3)
    add2(1, 2)
    add2(1, 3)
    for part in range(3):
        add3(1, part)
    spread(1, 0)
    finish(0)
    add3(1, 3)
    spread(1, 1)
    finish(1)

    for k in range(1, 8):
        meet(k).wait_send()
        leave(k).wait()
    for copy in (state_out, hidden_out, cot_out, pre_out):
        copy.wait_send()
    for n, buf in enumerate((state, hidden, cots)):
        halo_sent(n, buf, 0)
        halo_sent(n, buf, 1)
    for g in range(2):
        for part in range(4):
            for h in range(2):
                for half in range(2):
                    for j in range(3):
                        step1(g, part, h, half, j).wait_send()
                for k in (1, 2, 3):
                    step2(g, part, h, k).wait_send()
            for k in range(1, 8):
                step3(g, part, k).wait_send()
        for piece in range(2):
            for k, cross in every5:
                step5(g, piece, k, cross).wait_send()


def whole_step(state, truth, first, second):
    bf, f32 = jnp.bfloat16, jnp.float32
    dma = pltpu.SemaphoreType.DMA
    vmem = pltpu.VMEM
    block = vmem((6, 10, 16, 512), bf)
    scratch = [
        vmem((9, 512, 512), bf),
        vmem((9, 512, 512), bf),
        vmem((8, 2, 4, 8, 512), bf),
        vmem((4, 512, 128), f32),
        block,
        block,
        block,
        block,
        block,
        vmem((512, 512), f32),
        vmem((4, 512, 128), f32),
        vmem((8, 64, 512), bf),
        vmem((512, 512), bf),
        vmem((512, 512), bf),
        vmem((2, 512, 256), bf),
        vmem((4, 8, 512), bf),
        vmem((2, 256, 512), bf),
    ]
    for height in HEIGHT:
        scratch += [vmem((2, 4, 9, 4, height, 128), bf), vmem((2, 3, 9, 4, height, 128), bf)]
    for height in HEIGHT:
        scratch += [vmem((2, 4, 9, height, 128), bf), vmem((2, 3, 9, height, 128), bf)]
    scratch += [
        vmem((2, 2, 5, 16, 128), bf),
        vmem((2, 4, 5, 32, 128), bf),
        vmem((2, 8, 5, 32, 128), bf),
        vmem((2, 8, 5, 16, 128), bf),
    ]
    scratch += [dma((4,)), dma((4,)), dma((4,)), dma((3, 2, 8)), dma((3, 2, 8)), dma((2, 8)), dma((2, 8))]
    for dims in ((2, 16, 3), (2, 8, 4), (2, 4, 8), (2, 2, 8)):
        scratch += [dma(dims), dma(dims)]
    in_vmem = pl.BlockSpec(memory_space=pltpu.VMEM)
    return pl.pallas_call(
        step_kernel,
        out_shape=[jax.ShapeDtypeStruct((8, 64, 512), bf), jax.ShapeDtypeStruct((2, 9, 16, 512), bf)],
        in_specs=[pl.BlockSpec(memory_space=pl.ANY)] * 4,
        out_specs=[in_vmem] * 2,
        scratch_shapes=scratch,
        compiler_params=pltpu.CompilerParams(collective_id=0, has_side_effects=True, vmem_limit_bytes=60 << 20),
        name="whole_step",
    )(state, truth, first, second)


def body(state, truth, conv_first, conv_second):
    members, rows, cols, channels = state.shape
    prognosis, slopes = whole_step(
        state, truth, jnp.transpose(conv_first, (1, 0, 2)), jnp.transpose(conv_second, (1, 0, 2))
    )
    prognosis = prognosis.reshape(8, members, rows, cols // 8, channels).transpose(1, 2, 0, 3, 4).reshape(state.shape)
    second, first = [jnp.transpose(slopes[g], (1, 0, 2)).astype(jnp.float32) for g in range(2)]
    return prognosis, first, second


def solution(mesh):
    in_specs = (P("member", "rows", None, None), P("rows", None, None), P(), P())
    out_specs = (P("member", "rows", None, None), P("rows", None, None), P("rows", None, None))
    return jax.shard_map(body, mesh=mesh, in_specs=in_specs, out_specs=out_specs, check_vma=False)
```
